128 devices in a mesh: tm: 64 (over x, z, y), row: 2 (over core).
Axes of the slice: x: 4, y: 4, z: 4, core: 2. Of those that a mesh axis runs over, the one named last changes fastest.
Arguments:
- init_mean: float32 [1024], replicated, may hold values from -6 to 6
- jac_skew: bfloat16 [128, 1024, 1024], P('tm', 'row'), may hold values from -0.1875 to 0.1875
- gain_diag: float32 [1024], replicated, may hold values from 0.3 to 0.9
- gain_cross: float32 [1024, 1024], replicated, may hold values from -0.0234375 to 0.0234375
- smooth_diag: float32 [1024], replicated, may hold values from 0.2 to 0.8
- smooth_cross: float32 [1024, 1024], replicated, may hold values from -0.046875 to 0.046875
- obs_values: float32 [128, 128], P(('tm', 'row')), may hold values from -6 to 6
- obs_prec: float32 [128], P(('tm', 'row')), may hold values from 0.2 to 2
- obs_sensor: int32 [128], P(('tm', 'row')), may hold values from 0 to 511
- obs_block: int32 [128], P(('tm', 'row')), may hold values from 0 to 7
- sensor_step: int32 [512], replicated, may hold values from 0 to 127
Outputs:
- filtered: float32 [128, 1024], P('tm', 'row')
- smoothed: float32 [128, 1024], P('tm', 'row')
The draws below stay inside these ranges and needn't reach their ends.
All inputs are finite; a program needn't handle non-finite values.
Results may differ from the reference program's by a relative error of at most 0.0003.
Values may be sent and summed in bfloat16 or wider, within the bound.
A program may use at most 128 MiB of HBM per device.

```python
import math
import jax
import jax.numpy as jnp
from jax import lax

D = 1024
BLOCK = 128
STEPS_DEV = 2
STEPS = 128
OBS = 128
SENSORS = 512


def plant(result, rng, least, largest):
    longest = result.shape.index(max(result.shape))
    spots = []
    for shift in (0, 1):
        where = [jax.random.randint(jax.random.fold_in(rng, axis), (), 0, length) for axis, length in enumerate(result.shape)]
        where[longest] = (where[longest] + shift) % result.shape[longest]
        spots.append(tuple(where))
    return result.at[spots[0]].set(least).at[spots[1]].set(largest)


def steps_of(key, extent, shards, least, high):
    level = 1.0
    for position, shards_of in shards:
        heights = jax.random.uniform(jax.random.fold_in(jax.random.fold_in(key, 6), position), (shards_of,), jnp.float32, least / len(shards), high / len(shards))
        level = level * jnp.repeat(jnp.exp(heights), extent[position] // shards_of).reshape((-1,) + (1,) * (len(extent) - 1 - position))
    return level


def scatter_about(rng, shape, scale, limit, shards=(), kind=jnp.bfloat16):
    entries = jax.random.normal(rng, shape, jnp.float32) * scale
    if len(shards) > 0:
        entries = steps_of(rng, shape, shards, -0.22, 0.18) * entries
    return jnp.clip(entries, min=-limit, max=limit).astype(kind)


def setup_inputs(seed: int = 0) -> dict:
    arg_keys = jax.random.split(jax.random.key(seed), 12)
    init_mean = scatter_about(arg_keys[0], (D,), 1.0, 6.0, (), jnp.float32)
    jac_skew = scatter_about(arg_keys[1], (STEPS, D, D), D ** -0.5, 0.1875, ((0, 64), (1, 2)))
    gain_diag = jnp.clip(jnp.exp(jax.random.uniform(arg_keys[2], (D,), jnp.float32, math.log(0.3), math.log(0.9))), 0.3, 0.9)
    gain_cross = scatter_about(arg_keys[3], (D, D), (D * 64) ** -0.5, 0.0234375, (), jnp.float32)
    smooth_diag = jnp.clip(jnp.exp(jax.random.uniform(arg_keys[4], (D,), jnp.float32, math.log(0.2), math.log(0.8))), 0.2, 0.8)
    smooth_cross = scatter_about(arg_keys[5], (D, D), (D * 16) ** -0.5, 0.046875, (), jnp.float32)
    obs_values = scatter_about(arg_keys[6], (OBS, BLOCK), 1.0, 6.0, ((0, 128),), jnp.float32)
    obs_prec = jnp.clip(jnp.exp(math.log(2.0) - 2.3025851 * jax.random.uniform(arg_keys[7], (OBS,), jnp.float32) ** steps_of(arg_keys[7], (OBS,), ((0, 128),), -0.2, 0.2)), 0.2, 2.0)
    obs_sensor = plant(jax.random.randint(arg_keys[8], (OBS,), 0, SENSORS), jax.random.fold_in(arg_keys[8], 1), 0, SENSORS - 1).astype(jnp.int32)
    obs_block = plant(jax.random.randint(arg_keys[9], (OBS,), 0, D // BLOCK), jax.random.fold_in(arg_keys[9], 1), 0, (D // BLOCK) - 1).astype(jnp.int32)
    sensor_step = plant(jax.random.randint(arg_keys[10], (SENSORS,), 0, STEPS), jax.random.fold_in(arg_keys[10], 1), 0, STEPS - 1).astype(jnp.int32)
    return {"init_mean": init_mean, "jac_skew": jac_skew, "gain_diag": gain_diag, "gain_cross": gain_cross, "smooth_diag": smooth_diag, "smooth_cross": smooth_cross, "obs_values": obs_values, "obs_prec": obs_prec, "obs_sensor": obs_sensor, "obs_block": obs_block, "sensor_step": sensor_step}


step_length = 0.25
finest_accuracy = lax.Precision.HIGHEST


def tangent_map(skew_step, identity):
    skew_wide = skew_step.astype(jnp.float32)
    jacobian = skew_wide - skew_wide.T
    section = identity + (step_length / 4.0) * jacobian
    for divisor in (3.0, 2.0):
        section = identity + (step_length / divisor) * jnp.dot(section, jacobian, precision=finest_accuracy)
    return identity + step_length * jnp.dot(section, jacobian, precision=finest_accuracy)


def cell_totals(obs_values, obs_prec, obs_sensor, obs_block, sensor_step):
    obs_steps = sensor_step[obs_sensor]
    cell_index = (obs_steps * (D // BLOCK) + obs_block).astype(jnp.int32)
    weighted = obs_prec[:, None] * obs_values
    spread = jnp.broadcast_to(obs_prec[:, None], weighted.shape)
    value_sums = jax.ops.segment_sum(weighted, cell_index, num_segments=STEPS * (D // BLOCK))
    weight_sums = jax.ops.segment_sum(spread, cell_index, num_segments=STEPS * (D // BLOCK))
    return value_sums.reshape(STEPS, D), weight_sums.reshape(STEPS, D)


def reference(init_mean, jac_skew, gain_diag, gain_cross, smooth_diag, smooth_cross, obs_values, obs_prec, obs_sensor, obs_block, sensor_step):
    identity = jnp.eye(D, dtype=jnp.float32)
    entire_blend_matrix = gain_cross + jnp.diag(gain_diag)
    value_sums, weight_sums = cell_totals(obs_values, obs_prec, obs_sensor, obs_block, sensor_step)
    measured_share = weight_sums / (weight_sums + 1.0)
    goal_estimate = value_sums / (weight_sums + 1.0)

    def advance(present_estimate, inputs):
        skew_step, share_stride, arrival_instant = inputs
        jacobian_propagator = tangent_map(skew_step, identity)
        predicted_estimate = jnp.dot(jacobian_propagator, present_estimate, precision=finest_accuracy)
        update_correction = jnp.dot(entire_blend_matrix, arrival_instant - share_stride * predicted_estimate, precision=finest_accuracy)
        corrected_estimate = predicted_estimate + update_correction
        return corrected_estimate, (corrected_estimate, update_correction)

    _, (filtered, increments) = lax.scan(advance, init_mean, (jac_skew, measured_share, goal_estimate))
    smoother_gain = smooth_cross + jnp.diag(smooth_diag)
    padded = jnp.concatenate([increments, jnp.zeros((STEPS_DEV, D), jnp.float32)], axis=0)
    carried = jnp.zeros((STEPS, D), jnp.float32)
    for lag_steps in range(STEPS_DEV, 0, -1):
        carried = padded[lag_steps:lag_steps + STEPS] + jnp.dot(carried, smoother_gain.T, precision=finest_accuracy)
    smoothed = filtered + jnp.dot(carried, smoother_gain.T, precision=finest_accuracy)
    return filtered, smoothed
```

```python
import functools

import jax
import jax.numpy as jnp
from jax import lax
from jax.experimental import pallas as pl
from jax.experimental.pallas import tpu as pltpu
from jax.sharding import PartitionSpec as P

F32 = jnp.float32
BF16 = jnp.bfloat16
MESH = pl.DeviceIdType.MESH
STEP = 0.25
LANES = 128
VMEM_BYTES = 67043328


def split(value):
    high = value.astype(BF16)
    return high, (value - high.astype(F32)).astype(BF16)


def dot3(left_high, left_low, right_high, right_low):
    dot = functools.partial(jnp.dot, preferred_element_type=F32)
    return dot(left_high, right_low) + dot(left_low, right_high) + dot(left_high, right_high)


def eye_rows(first_row, rows, width):
    row = lax.broadcasted_iota(jnp.int32, (rows, width), 0) + first_row
    return (row == lax.broadcasted_iota(jnp.int32, (rows, width), 1)).astype(F32)


def matvec(tile, vectors, out_blocks, groups):
    rows = [[] for _ in vectors]
    for block in range(out_blocks):
        totals = [None] * len(vectors)
        for group in range(groups):
            entries = tile(block, group)
            for index, vector in enumerate(vectors):
                term = entries * vector[group : group + 1, :]
                totals[index] = term if totals[index] is None else totals[index] + term
        for index, total in enumerate(totals):
            rows[index].append(jnp.sum(total.T, axis=0, keepdims=True))
    return [jnp.concatenate(found, axis=0) for found in rows]


def matvec_loop(tile, vectors, outs, out_blocks, groups):
    def block_turn(block, carry):
        for index, row in enumerate(matvec(lambda _, group: tile(block, group), vectors, 1, groups)):
            outs[index][pl.ds(block, 1), :] = row
        return carry

    lax.fori_loop(0, out_blocks, block_turn, 0)


def square(ref):
    def tile(block, group):
        start = block * LANES if isinstance(block, int) else pl.multiple_of(block * LANES, LANES)
        return ref[pl.ds(start, LANES), pl.ds(group * LANES, LANES)]

    return tile


def pair_tile(high, low):
    def tile(block, group):
        where = (pl.ds(pl.multiple_of(block * LANES, LANES), LANES), pl.ds(group * LANES, LANES))
        return high[where].astype(F32) + low[where].astype(F32)

    return tile


def kernel(
    dims,
    skew,
    gain_cross,
    gain_diag,
    smooth_cross,
    smooth_diag,
    init,
    obs_own,
    filtered,
    smoothed,
    skew_own,
    skew_far,
    a_high,
    a_low,
    b_high,
    b_low,
    w_high,
    w_low,
    g_full,
    m_full,
    g_high,
    g_low,
    tangent,
    p_high,
    p_low,
    composed,
    obs,
    share_wide,
    share,
    goal,
    gain_goal,
    offset,
    arrived,
    outgoing,
    state,
    work,
    result_own,
    result_far,
    later,
    local_sem,
    skew_sem,
    map_sem,
    obs_send,
    obs_recv,
    chain_send,
    chain_recv,
    last_send,
    far_recv,
    later_recv,
):
    turn = lax.axis_index("tm")
    core = lax.axis_index("row")
    turns = lax.axis_size("tm")
    width = gain_cross.shape[0]
    half = width // 2
    other = 1 - core
    size_x, size_z, size_y = dims

    def at(turn_id, core_id):
        return dict(device_id=(turn_id, core_id), device_id_type=MESH)

    def ring_peers(size, stride):
        here = lax.rem(turn // stride, size)
        return [turn + (lax.rem(here + shift, size) - here) * stride for shift in range(1, size)]

    rings = [(size_y, 1), (size_z, size_y), (size_x, size_y * size_z)]

    own_copy = pltpu.make_async_copy(
        skew.at[core], skew_own.at[pl.ds(core * half, half)], local_sem.at[0]
    )
    own_copy.start()
    gain_copy = pltpu.make_async_copy(gain_cross, g_full, local_sem.at[1])
    gain_copy.start()
    smooth_copy = pltpu.make_async_copy(smooth_cross, m_full, local_sem.at[2])
    smooth_copy.start()

    barrier = pltpu.get_barrier_semaphore()
    count = 1
    pl.semaphore_signal(barrier, inc=1, **at(turn, other))
    for size, stride in rings:
        for peer in ring_peers(size, stride):
            pl.semaphore_signal(barrier, inc=1, **at(peer, core))
            count += 1

    @pl.when(turn > 0)
    def _():
        for target in range(2):
            pl.semaphore_signal(barrier, inc=1, **at(turn - 1, target))

    @pl.when(turn < turns - 1)
    def _():
        for target in range(2):
            pl.semaphore_signal(barrier, inc=1, **at(turn + 1, target))

    slot = turn * 2 + core
    obs[pl.ds(slot, 1)] = obs_own[...]
    ends = jnp.where(turn > 0, 2, 0) + jnp.where(turn < turns - 1, 2, 0)
    pl.semaphore_wait(barrier, count + ends)

    skew_send = pltpu.make_async_remote_copy(
        src_ref=skew.at[other],
        dst_ref=skew_own.at[pl.ds(core * half, half)],
        send_sem=skew_sem.at[0],
        recv_sem=skew_sem.at[1],
        **at(turn, other),
    )
    skew_send.start()

    sent = []

    def obs_copy(first, rows, target, core_id, index):
        place = obs.at[pl.ds(first, rows)]
        copy = pltpu.make_async_remote_copy(
            src_ref=place,
            dst_ref=place,
            send_sem=obs_send.at[index],
            recv_sem=obs_recv.at[index],
            **at(target, core_id),
        )
        copy.start()
        sent.append(copy)
        return copy

    def obs_ring(number):
        size, stride = rings[number]
        rows = 2 * stride
        first = turn // stride * rows
        copies = []
        for index, peer in enumerate(ring_peers(size, stride)):
            copies.append(obs_copy(first, rows, peer, core, 1 + 3 * number + index))
        return copies

    core_copies = [obs_copy(slot, 1, turn, other, 0)]

    gain_copy.wait()

    def gain_turn(block, carry):
        rows = pl.ds(pl.multiple_of(block * LANES, LANES), LANES)
        value = g_full[rows, :] + eye_rows(block * LANES, LANES, width) * jnp.concatenate(
            [gain_diag[group : group + 1, :] for group in range(width // LANES)], axis=1
        )
        g_high[rows, :], g_low[rows, :] = split(value)
        return carry

    lax.fori_loop(0, width // LANES, gain_turn, 0)
    for copy in core_copies:
        copy.wait()
    ring_copies = obs_ring(0)
    own_copy.wait()
    skew_send.wait()

    def skew_turn(block, carry):
        rows = pl.ds(pl.multiple_of(block * LANES, LANES), LANES)
        value = STEP * (skew_own[rows, :].astype(F32) - skew_own[:, rows].astype(F32).T)
        a_high[rows, :], a_low[rows, :] = split(value)
        return carry

    lax.fori_loop(0, width // LANES, skew_turn, 0)
    for copy in ring_copies:
        copy.wait()
    ring_copies = obs_ring(1)

    strip = 256

    def square_turn(block, carry):
        rows = pl.ds(pl.multiple_of(block * strip, strip), strip)
        value = dot3(a_high[rows, :], a_low[rows, :], a_high[...], a_low[...])
        b_high[rows, :], b_low[rows, :] = split(value)
        a_value = a_high[rows, :].astype(F32) + a_low[rows, :].astype(F32)
        w_value = 0.5 * eye_rows(block * strip, strip, width) + a_value / 6.0 + value / 24.0
        w_high[rows, :], w_low[rows, :] = split(w_value)
        return carry

    lax.fori_loop(0, width // strip // 2, square_turn, 0)
    for copy in ring_copies:
        copy.wait()
    ring_copies = obs_ring(2)
    lax.fori_loop(width // strip // 2, width // strip, square_turn, 0)
    for copy in ring_copies:
        copy.wait()

    meta = obs[:, 1, :].T
    weighted = obs[:, 0, :]
    blocks = width // LANES
    block_ids = lax.broadcasted_iota(jnp.int32, (blocks, LANES), 0).astype(F32)
    for index in range(2):
        step = (turn * 2 + index).astype(F32)
        chosen = jnp.where((meta[1:2, :] == step) & (meta[2:3, :] == block_ids), 1.0, 0.0)
        weight = jnp.sum(chosen * meta[0:1, :], axis=1, keepdims=True)
        value = jnp.dot(chosen, weighted, precision=lax.Precision.HIGHEST, preferred_element_type=F32)
        share[index] = jnp.broadcast_to(weight / (weight + 1.0), (blocks, LANES))
        goal[index] = value / (weight + 1.0)
    for group in range(blocks):
        share_wide[:, group * LANES : (group + 1) * LANES] = share[core]

    def tangent_turn(block, carry):
        rows = pl.ds(pl.multiple_of(block * strip, strip), strip)
        value = dot3(b_high[rows, :], b_low[rows, :], w_high[...], w_low[...])
        a_value = a_high[rows, :].astype(F32) + a_low[rows, :].astype(F32)
        value = eye_rows(block * strip, strip, width) + a_value + value
        tangent[rows, :] = value
        return carry

    lax.fori_loop(0, width // strip, tangent_turn, 0)

    def shared_turn(block, carry):
        rows = pl.ds(pl.multiple_of(block * LANES, LANES), LANES)
        value = tangent[rows, :] * share_wide[pl.ds(block, 1), :]
        w_high[rows, :], w_low[rows, :] = split(value)
        return carry

    lax.fori_loop(0, blocks, shared_turn, 0)

    def map_copy(block, part):
        ref = (p_high, p_low)[part]
        place = ref.at[core, pl.ds(pl.multiple_of(block * strip, strip), strip)]
        return pltpu.make_async_remote_copy(
            src_ref=place,
            dst_ref=place,
            send_sem=map_sem.at[0, part],
            recv_sem=map_sem.at[1, part],
            **at(turn, other),
        )

    def map_turn(block, carry):
        rows = pl.ds(pl.multiple_of(block * strip, strip), strip)

        @pl.when(block > 0)
        def _():
            map_copy(block - 1, 0).start()
            map_copy(block - 1, 1).start()

        value = tangent[rows, :] - dot3(g_high[rows, :], g_low[rows, :], w_high[...], w_low[...])
        p_high[core, rows, :], p_low[core, rows, :] = split(value)
        return carry

    lax.fori_loop(0, width // strip, map_turn, 0)

    gain_tile = square(g_full)
    matvec_loop(gain_tile, [goal[0], goal[1]], [gain_goal.at[0], gain_goal.at[1]], blocks, blocks)
    for index in range(2):
        gain_goal[index] += gain_diag[...] * goal[index]
    map_copy(width // strip - 1, 0).start()
    map_copy(width // strip - 1, 1).start()
    for part in range(2):
        ref = (p_high, p_low)[part]
        whole = pltpu.make_async_remote_copy(
            src_ref=ref.at[core],
            dst_ref=ref.at[other],
            send_sem=map_sem.at[0, part],
            recv_sem=map_sem.at[1, part],
            **at(turn, other),
        )
        whole.wait_send()
        whole.wait_recv()
    columns = pl.ds(pl.multiple_of(core * half, half), half)

    def compose_turn(block, carry):
        rows = pl.ds(pl.multiple_of(block * strip, strip), strip)
        composed[rows, :] = dot3(
            p_high[1, rows, :], p_low[1, rows, :], p_high[0, :, columns], p_low[0, :, columns]
        )
        return carry

    lax.fori_loop(0, width // strip, compose_turn, 0)
    matvec_loop(pair_tile(p_high.at[1], p_low.at[1]), [gain_goal[0]], [offset], blocks, blocks)
    offset[...] = jnp.where(core == 0, offset[...] + gain_goal[1], 0.0)

    @pl.when(turn == 0)
    def _():
        state[...] = init[...]

    @pl.when(turn > 0)
    def _():
        pltpu.make_async_copy(arrived, arrived, chain_recv).wait()
        state[...] = arrived[0] + arrived[1]

    @pl.when(turn < turns - 1)
    def _():
        own_half = state[pl.ds(core * (blocks // 2), blocks // 2), :]
        outgoing[...] = matvec(square(composed), [own_half], blocks, blocks // 2)[0] + offset[...]
        for target in range(2):
            pltpu.make_async_remote_copy(
                src_ref=outgoing,
                dst_ref=arrived.at[core],
                send_sem=chain_send.at[target],
                recv_sem=chain_recv,
                **at(turn + 1, target),
            ).start()

    @pl.when(core == 1)
    def _():
        matvec_loop(pair_tile(p_high.at[0], p_low.at[0]), [state[...]], [work.at[0]], blocks, blocks)
        state[...] = work[0] + gain_goal[0]

    matvec_loop(square(tangent), [state[...]], [work.at[0]], blocks, blocks)
    missing = goal[core] - share[core] * work[0]
    matvec_loop(gain_tile, [missing], [work.at[1]], blocks, blocks)
    increment = work[1] + gain_diag[...] * missing
    result_own[0] = increment
    result_own[1] = work[0] + increment

    far_copy = pltpu.make_async_remote_copy(
        src_ref=result_own,
        dst_ref=result_far,
        send_sem=last_send.at[2],
        recv_sem=far_recv,
        **at(turn, other),
    )

    def later_copy(target):
        return pltpu.make_async_remote_copy(
            src_ref=result_own.at[0],
            dst_ref=later.at[core],
            send_sem=last_send.at[target],
            recv_sem=later_recv,
            **at(turn - 1, target),
        )

    @pl.when(turn > 0)
    def _():
        later_copy(0).start()
        later_copy(1).start()

    far_copy.start()

    @pl.when(turn == turns - 1)
    def _():
        later[...] = jnp.zeros_like(later)

    far_copy.wait()
    smooth_copy.wait()

    @pl.when(turn < turns - 1)
    def _():
        pltpu.make_async_copy(later, later, later_recv).wait()

    smooth_tile = square(m_full)
    matvec_loop(smooth_tile, [later[0], later[1]], [work.at[0], work.at[1]], blocks, blocks)
    second = jnp.where(core == 1, result_own[0], result_far[0])
    first_carried = second + work[0] + smooth_diag[...] * later[0]
    second_carried = later[0] + work[1] + smooth_diag[...] * later[1]
    work[0] = first_carried
    work[1] = second_carried
    part = pl.ds(core * (blocks // 2), blocks // 2)

    def half_tile(block, group):
        start = pl.multiple_of(core * half + block * LANES, LANES)
        return m_full[pl.ds(start, LANES), pl.ds(group * LANES, LANES)]

    matvec_loop(
        half_tile, [first_carried, second_carried], [smoothed.at[0], smoothed.at[1]], blocks // 2, blocks
    )
    diag_part = smooth_diag[part, :]
    for index in range(2):
        mean = jnp.where(core == index, result_own[1, part, :], result_far[1, part, :])
        filtered[index] = mean
        smoothed[index] = mean + smoothed[index] + diag_part * work[index, part, :]

    @pl.when(turn < turns - 1)
    def _():
        for target in range(2):
            pltpu.make_async_remote_copy(
                src_ref=outgoing,
                dst_ref=arrived.at[core],
                send_sem=chain_send.at[target],
                recv_sem=chain_recv,
                **at(turn + 1, target),
            ).wait_send()

    @pl.when(turn > 0)
    def _():
        later_copy(0).wait_send()
        later_copy(1).wait_send()


def shards(
    dims,
    init_mean,
    jac_skew,
    gain_diag,
    gain_cross,
    smooth_diag,
    smooth_cross,
    obs_values,
    obs_prec,
    obs_sensor,
    obs_block,
    sensor_step,
):
    width = jac_skew.shape[2]
    blocks = width // LANES
    hits = obs_sensor[:, None] == jnp.arange(sensor_step.shape[0], dtype=jnp.int32)[None, :]
    obs_step = jnp.sum(jnp.where(hits, sensor_step[None, :], 0), axis=1).astype(F32)
    lane = jnp.arange(LANES, dtype=jnp.int32)[None, :]
    meta = jnp.where(
        lane == 0,
        obs_prec[:, None],
        jnp.where(lane == 1, obs_step[:, None], obs_block[:, None].astype(F32)),
    )
    obs_own = jnp.stack([obs_prec[:, None] * obs_values, meta], axis=1)
    obs_total = lax.axis_size(("tm", "row"))
    vmem = pl.BlockSpec(memory_space=pltpu.VMEM)
    hbm = pl.BlockSpec(memory_space=pltpu.HBM)

    def wide(kind, lead=(), columns=width):
        return pltpu.VMEM(tuple(lead) + (width, columns), kind)

    def small(*lead):
        return pltpu.VMEM(tuple(lead) + (blocks, LANES), F32)

    dma = pltpu.SemaphoreType.DMA
    filtered, smoothed = pl.pallas_call(
        functools.partial(kernel, dims),
        out_shape=[jax.ShapeDtypeStruct((2, blocks // 2, LANES), F32)] * 2,
        in_specs=[hbm, hbm, vmem, hbm, vmem, vmem, vmem],
        out_specs=[vmem, vmem],
        scratch_shapes=[
            wide(BF16),
            pltpu.VMEM((8, LANES), F32),
            wide(BF16),
            wide(BF16),
            wide(BF16),
            wide(BF16),
            wide(BF16),
            wide(BF16),
            wide(F32),
            wide(F32),
            wide(BF16),
            wide(BF16),
            wide(F32),
            wide(BF16, (2,)),
            wide(BF16, (2,)),
            wide(F32, (), width // 2),
            pltpu.VMEM((obs_total, 2, LANES), F32),
            pltpu.VMEM((blocks, width), F32),
            small(2),
            small(2),
            small(2),
            small(),
            small(2),
            small(),
            small(),
            small(2),
            small(2),
            small(2),
            small(2),
            dma((3,)),
            dma((2,)),
            dma((2, 2)),
            dma((10,)),
            dma((10,)),
            dma((2,)),
            dma,
            dma((3,)),
            dma,
            dma,
        ],
        compiler_params=pltpu.CompilerParams(
            collective_id=0, has_side_effects=True, vmem_limit_bytes=VMEM_BYTES
        ),
    )(
        jac_skew,
        gain_cross,
        gain_diag.reshape(blocks, LANES),
        smooth_cross,
        smooth_diag.reshape(blocks, LANES),
        init_mean.reshape(blocks, LANES),
        obs_own,
    )
    return filtered.reshape(2, width // 2), smoothed.reshape(2, width // 2)


def solution(mesh):
    turns = mesh.shape["tm"]
    dims = {64: (4, 4, 4), 4: (1, 2, 2), 8: (2, 2, 2)}[turns]
    in_specs = (
        P(),
        P("tm", "row", None),
        P(),
        P(),
        P(),
        P(),
        P(("tm", "row"), None),
        P(("tm", "row")),
        P(("tm", "row")),
        P(("tm", "row")),
        P(),
    )
    out_specs = (P("tm", "row"), P("tm", "row"))
    return jax.shard_map(
        functools.partial(shards, dims),
        mesh=mesh,
        in_specs=in_specs,
        out_specs=out_specs,
        check_vma=False,
    )
```

```python
import functools

import jax
import jax.numpy as jnp
from jax import lax
from jax.experimental import pallas as pl
from jax.experimental.pallas import tpu as pltpu
from jax.sharding import PartitionSpec as P

F32 = jnp.float32
BF16 = jnp.bfloat16
MESH = pl.DeviceIdType.MESH
STEP = 0.25
LANES = 128
VMEM_BYTES = 67043328
LEVELS = 32767.0
dot = functools.partial(jnp.dot, preferred_element_type=F32)


def split(value):
    high = value.astype(BF16)
    return high, (value - high.astype(F32)).astype(BF16)


def dot3(left_high, left_low, right_high, right_low):
    return dot(left_high, right_low) + dot(left_low, right_high) + dot(left_high, right_high)


def eye_rows(first_row, rows, width):
    row = lax.broadcasted_iota(jnp.int32, (rows, width), 0) + first_row
    return (row == lax.broadcasted_iota(jnp.int32, (rows, width), 1)).astype(F32)


def matvec(tile, vectors, out_blocks, groups):
    rows = [[] for _ in vectors]
    for block in range(out_blocks):
        totals = [None] * len(vectors)
        for group in range(groups):
            entries = tile(block, group)
            for index, vector in enumerate(vectors):
                term = entries * vector[group : group + 1, :]
                totals[index] = term if totals[index] is None else totals[index] + term
        for index, total in enumerate(totals):
            rows[index].append(jnp.sum(total.T, axis=0, keepdims=True))
    return [jnp.concatenate(found, axis=0) for found in rows]


def matvec_loop(tile, vectors, outs, out_blocks, groups):
    def block_turn(block, carry):
        for index, row in enumerate(matvec(lambda _, group: tile(block, group), vectors, 1, groups)):
            outs[index][pl.ds(block, 1), :] = row
        return carry

    lax.fori_loop(0, out_blocks, block_turn, 0)


def square(ref):
    def tile(block, group):
        start = block * LANES if isinstance(block, int) else pl.multiple_of(block * LANES, LANES)
        return ref[pl.ds(start, LANES), pl.ds(group * LANES, LANES)]

    return tile


def pair_tile(high, low):
    def tile(block, group):
        where = (pl.ds(pl.multiple_of(block * LANES, LANES), LANES), pl.ds(group * LANES, LANES))
        return high[where].astype(F32) + low[where].astype(F32)

    return tile


def kernel(
    dims,
    skew,
    gain_cross,
    gain_diag,
    smooth_cross,
    smooth_diag,
    init,
    obs_values,
    obs_prec,
    obs_sensor,
    obs_block,
    sensor_step,
    filtered,
    smoothed,
    skew_own,
    a_high,
    a_low,
    b_high,
    b_low,
    w_high,
    w_low,
    g_full,
    m_full,
    g_high,
    g_low,
    tangent,
    p_high,
    p_low,
    composed,
    c_high,
    c_low,
    prefix,
    coded_in,
    coded_out,
    scales_in,
    scales_out,
    obs,
    share_wide,
    share,
    goal,
    gain_goal,
    offset,
    offset_in,
    partial_out,
    partial_in,
    arrived,
    outgoing,
    state,
    work,
    result_own,
    result_far,
    later,
    summed,
    local_sem,
    skew_sem,
    map_sem,
    obs_send,
    obs_recv,
    whole_sem,
    block_send,
    block_recv,
    offset_sem,
    partial_sem,
    chain_send,
    chain_recv,
    last_send,
    far_recv,
    later_recv,
):
    turn = lax.axis_index("tm")
    core = lax.axis_index("row")
    turns = lax.axis_size("tm")
    width = gain_cross.shape[0]
    half = width // 2
    other = 1 - core
    size_x, size_z, size_y = dims
    blocks = width // LANES
    parts = half // LANES
    group = size_y
    front = min(3, size_x * size_z - 1) * group
    place = lax.rem(turn, group)
    streams = turn >= front
    source = jnp.where(streams, turn - place, turn) - 1
    sends_one = turn < front - 1
    sends_all = (turn == front - 1) | (streams & (place == group - 1) & (turn < turns - 1))
    follows = streams & (place > 0)
    leads = streams & (place == 0)

    def at(turn_id, core_id):
        return dict(device_id=(turn_id, core_id), device_id_type=MESH)

    def ring_peers(size, stride):
        here = lax.rem(turn // stride, size)
        return [turn + (lax.rem(here + shift, size) - here) * stride for shift in range(1, size)]

    rings = [(size_y, 1), (size_z, size_y), (size_x, size_y * size_z)]

    own_copy = pltpu.make_async_copy(
        skew.at[core], skew_own.at[pl.ds(core * half, half)], local_sem.at[0]
    )
    own_copy.start()
    gain_copy = pltpu.make_async_copy(gain_cross, g_full, local_sem.at[1])
    gain_copy.start()
    smooth_copy = pltpu.make_async_copy(smooth_cross, m_full, local_sem.at[2])
    smooth_copy.start()

    barrier = pltpu.get_barrier_semaphore()
    count = 1
    pl.semaphore_signal(barrier, inc=1, **at(turn, other))
    for size, stride in rings:
        for peer in ring_peers(size, stride):
            pl.semaphore_signal(barrier, inc=1, **at(peer, core))
            count += 1

    @pl.when(turn > 0)
    def _():
        for target in range(2):
            pl.semaphore_signal(barrier, inc=1, **at(source, target))

    @pl.when(turn < turns - 1)
    def _():
        for target in range(2):
            pl.semaphore_signal(barrier, inc=1, **at(turn + 1, target))

    slot = turn * 2 + core
    sensor_ids = lax.broadcasted_iota(jnp.int32, sensor_step.shape, 0) * LANES
    sensor_ids += lax.broadcasted_iota(jnp.int32, sensor_step.shape, 1)
    found = jnp.where(sensor_ids == obs_sensor[0], sensor_step[...], 0).astype(F32)
    found = jnp.sum(jnp.sum(found, axis=0, keepdims=True), axis=1, keepdims=True)
    lane = lax.broadcasted_iota(jnp.int32, (1, LANES), 1)
    meta_row = jnp.where(
        lane == 0, obs_prec[0], jnp.where(lane == 1, found, obs_block[0].astype(F32))
    )
    obs[slot, 0:1, :] = obs_prec[0] * obs_values[...]
    obs[slot, 1:2, :] = meta_row
    ends = jnp.where(turn > 0, 2, 0) + jnp.where(sends_one, 2, 0)
    ends += jnp.where(sends_all, 2 * group, 0)
    pl.semaphore_wait(barrier, count + ends)

    skew_send = pltpu.make_async_remote_copy(
        src_ref=skew.at[other],
        dst_ref=skew_own.at[pl.ds(core * half, half)],
        send_sem=skew_sem.at[0],
        recv_sem=skew_sem.at[1],
        **at(turn, other),
    )
    skew_send.start()

    sent = []

    def obs_copy(first, rows, target, core_id, index):
        rows_ref = obs.at[pl.ds(first, rows)]
        copy = pltpu.make_async_remote_copy(
            src_ref=rows_ref,
            dst_ref=rows_ref,
            send_sem=obs_send.at[index],
            recv_sem=obs_recv.at[index],
            **at(target, core_id),
        )
        copy.start()
        sent.append(copy)
        return copy

    def obs_ring(number):
        size, stride = rings[number]
        rows = 2 * stride
        first = turn // stride * rows
        copies = []
        for index, peer in enumerate(ring_peers(size, stride)):
            copies.append(obs_copy(first, rows, peer, core, 1 + 3 * number + index))
        return copies

    core_copies = [obs_copy(slot, 1, turn, other, 0)]

    gain_copy.wait()

    def gain_turn(block, carry):
        rows = pl.ds(pl.multiple_of(block * LANES, LANES), LANES)
        value = g_full[rows, :] + eye_rows(block * LANES, LANES, width) * jnp.concatenate(
            [gain_diag[group : group + 1, :] for group in range(width // LANES)], axis=1
        )
        g_high[rows, :], g_low[rows, :] = split(value)
        return carry

    lax.fori_loop(0, width // LANES, gain_turn, 0)
    for copy in core_copies:
        copy.wait()
    ring_copies = obs_ring(0)
    own_copy.wait()
    skew_send.wait()

    def skew_turn(block, carry):
        rows = pl.ds(pl.multiple_of(block * LANES, LANES), LANES)
        value = STEP * (skew_own[rows, :].astype(F32) - skew_own[:, rows].astype(F32).T)
        a_high[rows, :], a_low[rows, :] = split(value)
        return carry

    lax.fori_loop(0, width // LANES, skew_turn, 0)
    for copy in ring_copies:
        copy.wait()
    ring_copies = obs_ring(1)

    strip = 256

    def square_turn(block, carry):
        rows = pl.ds(pl.multiple_of(block * strip, strip), strip)
        value = dot3(a_high[rows, :], a_low[rows, :], a_high[...], a_low[...])
        b_high[rows, :], b_low[rows, :] = split(value)
        a_value = a_high[rows, :].astype(F32) + a_low[rows, :].astype(F32)
        w_value = 0.5 * eye_rows(block * strip, strip, width) + a_value / 6.0 + value / 24.0
        w_high[rows, :], w_low[rows, :] = split(w_value)
        return carry

    lax.fori_loop(0, width // strip // 2, square_turn, 0)
    for copy in ring_copies:
        copy.wait()
    ring_copies = obs_ring(2)
    lax.fori_loop(width // strip // 2, width // strip, square_turn, 0)
    for copy in ring_copies:
        copy.wait()

    meta = obs[:, 1, :].T
    weighted = obs[:, 0, :]
    block_ids = lax.broadcasted_iota(jnp.int32, (blocks, LANES), 0).astype(F32)
    for index in range(2):
        step = (turn * 2 + index).astype(F32)
        chosen = jnp.where((meta[1:2, :] == step) & (meta[2:3, :] == block_ids), 1.0, 0.0)
        weight = jnp.sum(chosen * meta[0:1, :], axis=1, keepdims=True)
        value = jnp.dot(chosen, weighted, precision=lax.Precision.HIGHEST, preferred_element_type=F32)
        share[index] = jnp.broadcast_to(weight / (weight + 1.0), (blocks, LANES))
        goal[index] = value / (weight + 1.0)
    for column in range(blocks):
        share_wide[:, column * LANES : (column + 1) * LANES] = share[core]

    def tangent_turn(block, carry):
        rows = pl.ds(pl.multiple_of(block * strip, strip), strip)
        value = dot3(b_high[rows, :], b_low[rows, :], w_high[...], w_low[...])
        a_value = a_high[rows, :].astype(F32) + a_low[rows, :].astype(F32)
        value = eye_rows(block * strip, strip, width) + a_value + value
        tangent[rows, :] = value
        return carry

    lax.fori_loop(0, width // strip, tangent_turn, 0)

    def shared_turn(block, carry):
        rows = pl.ds(pl.multiple_of(block * LANES, LANES), LANES)
        value = tangent[rows, :] * share_wide[pl.ds(block, 1), :]
        w_high[rows, :], w_low[rows, :] = split(value)
        return carry

    lax.fori_loop(0, blocks, shared_turn, 0)

    def map_copy(block, part):
        ref = (p_high, p_low)[part]
        strip_ref = ref.at[core, pl.ds(pl.multiple_of(block * strip, strip), strip)]
        return pltpu.make_async_remote_copy(
            src_ref=strip_ref,
            dst_ref=strip_ref,
            send_sem=map_sem.at[0, part],
            recv_sem=map_sem.at[1, part],
            **at(turn, other),
        )

    def map_turn(block, carry):
        rows = pl.ds(pl.multiple_of(block * strip, strip), strip)

        @pl.when(block > 0)
        def _():
            map_copy(block - 1, 0).start()
            map_copy(block - 1, 1).start()

        value = tangent[rows, :] - dot3(g_high[rows, :], g_low[rows, :], w_high[...], w_low[...])
        p_high[core, rows, :], p_low[core, rows, :] = split(value)
        return carry

    lax.fori_loop(0, width // strip, map_turn, 0)

    gain_tile = square(g_full)
    matvec_loop(gain_tile, [goal[0], goal[1]], [gain_goal.at[0], gain_goal.at[1]], blocks, blocks)
    for index in range(2):
        gain_goal[index] += gain_diag[...] * goal[index]
    map_copy(width // strip - 1, 0).start()
    map_copy(width // strip - 1, 1).start()
    for part in range(2):
        ref = (p_high, p_low)[part]
        whole = pltpu.make_async_remote_copy(
            src_ref=ref.at[core],
            dst_ref=ref.at[other],
            send_sem=map_sem.at[0, part],
            recv_sem=map_sem.at[1, part],
            **at(turn, other),
        )
        whole.wait_send()
        whole.wait_recv()

    def eye_block(block):
        row = lax.broadcasted_iota(jnp.int32, (width, LANES), 0) - (core * half + block * LANES)
        return row == lax.broadcasted_iota(jnp.int32, (width, LANES), 1)

    def block_copies(block):
        return [
            pltpu.make_async_remote_copy(
                src_ref=out_ref.at[block],
                dst_ref=in_ref.at[block],
                send_sem=block_send.at[block, index],
                recv_sem=block_recv.at[block, index],
                **at(turn + 1, core),
            )
            for index, (out_ref, in_ref) in enumerate(
                ((coded_out, coded_in), (scales_out, scales_in))
            )
        ]

    def send_block(value, block):
        diagonal = eye_block(block)
        rest = jnp.where(diagonal, 0.0, value)
        largest = jnp.max(jnp.abs(rest), axis=0, keepdims=True)
        factor = jnp.where(largest > 1e-30, LEVELS / jnp.maximum(largest, 1e-30), 0.0)
        coded_out[block] = jnp.round(rest * factor).astype(jnp.int32).astype(jnp.int16)
        scales_out[block, 0:1, :] = largest * (1.0 / LEVELS)
        scales_out[block, 1:2, :] = jnp.sum(value - rest, axis=0, keepdims=True)
        for copy in block_copies(block):
            copy.start()

    def product(left_high, left_low, right_high, right_low):
        both = dot(left_high, jnp.concatenate([right_high, right_low], axis=1))
        return (both[:, LANES:] + dot(left_low, right_high)) + both[:, :LANES]

    def lane_block(start):
        return pl.ds(pl.multiple_of(start, LANES), LANES)

    def compose_turn(block, carry):
        columns = lane_block(core * half + block * LANES)
        own = lane_block(block * LANES)
        value = product(p_high[1], p_low[1], p_high[0, :, columns], p_low[0, :, columns])
        composed[:, own] = value
        c_high[core, :, own], c_low[core, :, own] = split(value)

        @pl.when(leads)
        def _():
            send_block(value, block)

        return carry

    lax.fori_loop(0, parts, compose_turn, 0)
    whole_copies = [
        pltpu.make_async_remote_copy(
            src_ref=ref.at[core],
            dst_ref=ref.at[core],
            send_sem=whole_sem.at[0, index],
            recv_sem=whole_sem.at[1, index],
            **at(turn, other),
        )
        for index, ref in enumerate((c_high, c_low))
    ]

    @pl.when(follows)
    def _():
        for copy in whole_copies:
            copy.start()

    matvec_loop(pair_tile(p_high.at[1], p_low.at[1]), [gain_goal[0]], [offset], blocks, blocks)
    offset[...] += gain_goal[1]
    offset_copy = pltpu.make_async_remote_copy(
        src_ref=offset,
        dst_ref=offset_in,
        send_sem=offset_sem.at[0],
        recv_sem=offset_sem.at[1],
        **at(turn + 1, core),
    )

    @pl.when(leads)
    def _():
        offset_copy.start()

    @pl.when(follows)
    def _():
        for copy in whole_copies:
            copy.wait()

        def stream_turn(block, carry):
            own = lane_block(block * LANES)
            for copy in block_copies(block):
                copy.wait_recv()
            value = coded_in[block].astype(jnp.int32).astype(F32) * scales_in[block, 0:1, :]
            value += jnp.where(eye_block(block), scales_in[block, 1:2, :], 0.0)
            prefix[:, own] = value
            high, low = split(value)
            value = product(c_high[0], c_low[0], high[:half], low[:half])
            value += product(c_high[1], c_low[1], high[half:], low[half:])

            @pl.when(place < group - 1)
            def _():
                send_block(value, block)

            @pl.when(place == group - 1)
            def _():
                composed[:, own] = value

            return carry

        lax.fori_loop(0, parts, stream_turn, 0)
        offset_copy.wait_recv()

        def whole_tile(block, column):
            rows = pl.ds(pl.multiple_of(block * LANES, LANES), LANES)
            where = (column // parts, rows, pl.ds(column % parts * LANES, LANES))
            return c_high[where].astype(F32) + c_low[where].astype(F32)

        matvec_loop(whole_tile, [offset_in[...]], [work.at[0]], blocks, blocks)
        offset[...] += work[0]

        @pl.when(place < group - 1)
        def _():
            offset_copy.start()

    @pl.when(turn == 0)
    def _():
        state[...] = init[...]

    @pl.when(turn > 0)
    def _():
        pltpu.make_async_copy(arrived, arrived, chain_recv).wait()
        state[...] = arrived[0] + arrived[1]

    own_half = pl.ds(core * parts, parts)

    def chain_copies(count):
        order = [count - 1] + list(range(count - 1))
        return [
            pltpu.make_async_remote_copy(
                src_ref=outgoing,
                dst_ref=arrived.at[core],
                send_sem=chain_send.at[2 * step + target],
                recv_sem=chain_recv,
                **at(turn + 1 + step, target),
            )
            for step in order
            for target in range(2)
        ]

    @pl.when(sends_one | sends_all)
    def _():
        moved = matvec(square(composed), [state[own_half, :]], blocks, parts)[0]
        outgoing[...] = moved + jnp.where(core == 0, offset[...], 0.0)

    @pl.when(sends_one)
    def _():
        for copy in chain_copies(1):
            copy.start()

    @pl.when(sends_all)
    def _():
        for copy in chain_copies(group):
            copy.start()

    partial_copy = pltpu.make_async_remote_copy(
        src_ref=partial_out,
        dst_ref=partial_in,
        send_sem=partial_sem.at[0],
        recv_sem=partial_sem.at[1],
        **at(turn, other),
    )

    @pl.when(follows)
    def _():
        moved = matvec(square(prefix), [state[own_half, :]], blocks, parts)[0]
        partial_out[...] = moved + jnp.where(core == 0, offset_in[...], 0.0)
        partial_copy.start()
        partial_copy.wait()
        state[...] = partial_out[...] + partial_in[...]

    @pl.when(core == 1)
    def _():
        matvec_loop(pair_tile(p_high.at[0], p_low.at[0]), [state[...]], [work.at[0]], blocks, blocks)
        state[...] = work[0] + gain_goal[0]

    matvec_loop(square(tangent), [state[...]], [work.at[0]], blocks, blocks)
    missing = goal[core] - share[core] * work[0]
    matvec_loop(gain_tile, [missing], [work.at[1]], blocks, blocks)
    increment = work[1] + gain_diag[...] * missing
    result_own[0] = increment
    result_own[1] = work[0] + increment

    far_copy = pltpu.make_async_remote_copy(
        src_ref=result_own,
        dst_ref=result_far,
        send_sem=last_send.at[2],
        recv_sem=far_recv,
        **at(turn, other),
    )

    def later_copy(target):
        return pltpu.make_async_remote_copy(
            src_ref=result_own.at[0],
            dst_ref=later.at[core],
            send_sem=last_send.at[target],
            recv_sem=later_recv,
            **at(turn - 1, target),
        )

    @pl.when(turn > 0)
    def _():
        later_copy(0).start()
        later_copy(1).start()

    far_copy.start()

    @pl.when(turn == turns - 1)
    def _():
        later[...] = jnp.zeros_like(later)

    far_copy.wait()
    smooth_copy.wait()

    @pl.when(turn < turns - 1)
    def _():
        pltpu.make_async_copy(later, later, later_recv).wait()

    smooth_tile = square(m_full)
    matvec_loop(smooth_tile, [later[0], later[1]], [work.at[0], work.at[1]], blocks, blocks)
    second = jnp.where(core == 1, result_own[0], result_far[0])
    first_carried = second + work[0] + smooth_diag[...] * later[0]
    second_carried = later[0] + work[1] + smooth_diag[...] * later[1]
    work[0] = first_carried
    work[1] = second_carried
    part = pl.ds(core * (blocks // 2), blocks // 2)

    def half_tile(block, group):
        start = pl.multiple_of(core * half + block * LANES, LANES)
        return m_full[pl.ds(start, LANES), pl.ds(group * LANES, LANES)]

    matvec_loop(
        half_tile, [first_carried, second_carried], [summed.at[0], summed.at[1]], blocks // 2, blocks
    )
    diag_part = smooth_diag[part, :]
    for index in range(2):
        mean = jnp.where(core == index, result_own[1, part, :], result_far[1, part, :])
        late = mean + summed[index] + diag_part * work[index, part, :]
        for column in range(blocks // 2):
            where = (pl.ds(index, 1), pl.ds(column * LANES, LANES))
            filtered[where] = mean[column : column + 1, :]
            smoothed[where] = late[column : column + 1, :]

    @pl.when(leads | (follows & (place < group - 1)))
    def _():
        for block in range(parts):
            for copy in block_copies(block):
                copy.wait_send()
        offset_copy.wait_send()

    @pl.when(sends_one)
    def _():
        for copy in chain_copies(1):
            copy.wait_send()

    @pl.when(sends_all)
    def _():
        for copy in chain_copies(group):
            copy.wait_send()

    @pl.when(turn > 0)
    def _():
        later_copy(0).wait_send()
        later_copy(1).wait_send()


def shards(
    dims,
    init_mean,
    jac_skew,
    gain_diag,
    gain_cross,
    smooth_diag,
    smooth_cross,
    obs_values,
    obs_prec,
    obs_sensor,
    obs_block,
    sensor_step,
):
    width = jac_skew.shape[2]
    blocks = width // LANES
    obs_total = lax.axis_size(("tm", "row"))
    vmem = pl.BlockSpec(memory_space=pltpu.VMEM)
    smem = pl.BlockSpec(memory_space=pltpu.SMEM)
    hbm = pl.BlockSpec(memory_space=pltpu.HBM)
    parts = blocks // 2
    group = dims[2]

    def wide(kind, lead=(), columns=width):
        return pltpu.VMEM(tuple(lead) + (width, columns), kind)

    def small(*lead):
        return pltpu.VMEM(tuple(lead) + (blocks, LANES), F32)

    dma = pltpu.SemaphoreType.DMA
    filtered, smoothed = pl.pallas_call(
        functools.partial(kernel, dims),
        out_shape=[jax.ShapeDtypeStruct((2, width // 2), F32)] * 2,
        in_specs=[hbm, hbm, vmem, hbm, vmem, vmem, vmem, smem, smem, smem, vmem],
        out_specs=[vmem, vmem],
        scratch_shapes=[
            wide(BF16),
            wide(BF16),
            wide(BF16),
            wide(BF16),
            wide(BF16),
            wide(BF16),
            wide(BF16),
            wide(F32),
            wide(F32),
            wide(BF16),
            wide(BF16),
            wide(F32),
            wide(BF16, (2,)),
            wide(BF16, (2,)),
            wide(F32, (), width // 2),
            wide(BF16, (2,), width // 2),
            wide(BF16, (2,), width // 2),
            wide(F32, (), width // 2),
            wide(jnp.int16, (parts,), LANES),
            wide(jnp.int16, (parts,), LANES),
            pltpu.VMEM((parts, 2, LANES), F32),
            pltpu.VMEM((parts, 2, LANES), F32),
            pltpu.VMEM((obs_total, 2, LANES), F32),
            pltpu.VMEM((blocks, width), F32),
            small(2),
            small(2),
            small(2),
            small(),
            small(),
            small(),
            small(),
            small(2),
            small(),
            small(),
            small(2),
            small(2),
            small(2),
            small(2),
            pltpu.VMEM((2, parts, LANES), F32),
            dma((3,)),
            dma((2,)),
            dma((2, 2)),
            dma((10,)),
            dma((10,)),
            dma((2, 2)),
            dma((parts, 2)),
            dma((parts, 2)),
            dma((2,)),
            dma((2,)),
            dma((2 * group,)),
            dma,
            dma((3,)),
            dma,
            dma,
        ],
        compiler_params=pltpu.CompilerParams(
            collective_id=0, has_side_effects=True, vmem_limit_bytes=VMEM_BYTES
        ),
    )(
        jac_skew,
        gain_cross,
        gain_diag.reshape(blocks, LANES),
        smooth_cross,
        smooth_diag.reshape(blocks, LANES),
        init_mean.reshape(blocks, LANES),
        obs_values,
        obs_prec,
        obs_sensor,
        obs_block,
        sensor_step.reshape(-1, LANES),
    )
    return filtered, smoothed


def solution(mesh):
    turns = mesh.shape["tm"]
    dims = {64: (4, 4, 4), 4: (1, 2, 2), 8: (2, 2, 2)}[turns]
    in_specs = (
        P(),
        P("tm", "row", None),
        P(),
        P(),
        P(),
        P(),
        P(("tm", "row"), None),
        P(("tm", "row")),
        P(("tm", "row")),
        P(("tm", "row")),
        P(),
    )
    out_specs = (P("tm", "row"), P("tm", "row"))
    return jax.shard_map(
        functools.partial(shards, dims),
        mesh=mesh,
        in_specs=in_specs,
        out_specs=out_specs,
        check_vma=False,
    )
```

```python
import functools

import jax
import jax.numpy as jnp
from jax import lax
from jax.experimental import pallas as pl
from jax.experimental.pallas import tpu as pltpu
from jax.sharding import PartitionSpec as P

F32 = jnp.float32
BF16 = jnp.bfloat16
MESH = pl.DeviceIdType.MESH
STEP = 0.25
LANES = 128
VMEM_BYTES = 67043328
LEVELS = 32767.0
CHUNK = 64
UNROLL = 4
dot = functools.partial(jnp.dot, preferred_element_type=F32)


def split(value):
    high = value.astype(BF16)
    return high, (value - high.astype(F32)).astype(BF16)


def dot3(left_high, left_low, right_high, right_low):
    return dot(left_high, right_low) + dot(left_low, right_high) + dot(left_high, right_high)


def eye_rows(first_row, rows, width):
    row = lax.broadcasted_iota(jnp.int32, (rows, width), 0) + first_row
    return (row == lax.broadcasted_iota(jnp.int32, (rows, width), 1)).astype(F32)


def matvec(tile, vectors, out_blocks, groups):
    rows = [[] for _ in vectors]
    for block in range(out_blocks):
        totals = [None] * len(vectors)
        for group in range(groups):
            entries = tile(block, group)
            for index, vector in enumerate(vectors):
                term = entries * vector[group : group + 1, :]
                totals[index] = term if totals[index] is None else totals[index] + term
        for index, total in enumerate(totals):
            rows[index].append(jnp.sum(total.T, axis=0, keepdims=True))
    return [jnp.concatenate(found, axis=0) for found in rows]


def matvec_loop(tile, vectors, outs, out_blocks, groups):
    def block_turn(turn, carry):
        first = turn * UNROLL
        found = matvec(lambda block, group: tile(first + block, group), vectors, UNROLL, groups)
        for index, rows in enumerate(found):
            for block in range(UNROLL):
                outs[index][pl.ds(first + block, 1), :] = rows[block : block + 1]
        return carry

    lax.fori_loop(0, out_blocks // UNROLL, block_turn, 0)


def square(ref):
    def tile(block, group):
        start = block * LANES if isinstance(block, int) else pl.multiple_of(block * LANES, LANES)
        return ref[pl.ds(start, LANES), pl.ds(group * LANES, LANES)]

    return tile


def pair_tile(high, low):
    def tile(block, group):
        where = (pl.ds(pl.multiple_of(block * LANES, LANES), LANES), pl.ds(group * LANES, LANES))
        return high[where].astype(F32) + low[where].astype(F32)

    return tile


def kernel(
    dims,
    skew,
    gain_cross,
    gain_diag,
    smooth_cross,
    smooth_diag,
    init,
    obs_values,
    obs_prec,
    obs_sensor,
    obs_block,
    sensor_step,
    result,
    skew_own,
    a_high,
    a_low,
    b_high,
    b_low,
    w_high,
    w_low,
    g_full,
    m_full,
    g_high,
    g_low,
    tangent,
    p_high,
    p_low,
    composed,
    c_high,
    c_low,
    prefix,
    coded_in,
    coded_out,
    scales_in,
    scales_out,
    turned_in,
    turned_out,
    obs,
    share_wide,
    share,
    goal,
    gain_goal,
    offset,
    offset_in,
    partial_out,
    partial_in,
    arrived,
    outgoing,
    state,
    work,
    result_own,
    result_far,
    later,
    summed,
    local_sem,
    skew_sem,
    map_sem,
    obs_send,
    obs_recv,
    whole_sem,
    block_send,
    block_recv,
    offset_sem,
    partial_sem,
    chain_send,
    chain_recv,
    last_send,
    far_recv,
    later_recv,
):
    turn = lax.axis_index("tm")
    core = lax.axis_index("row")
    turns = lax.axis_size("tm")
    width = gain_cross.shape[0]
    half = width // 2
    other = 1 - core
    size_x, size_z, size_y = dims
    blocks = width // LANES
    parts = half // LANES
    chunks = half // CHUNK
    group = size_y
    front = min(3, size_x * size_z - 1) * group
    place = lax.rem(turn, group)
    streams = turn >= front
    source = jnp.where(streams, turn - place, turn) - 1
    sends_one = turn < front - 1
    sends_all = (turn == front - 1) | (streams & (place == group - 1) & (turn < turns - 1))
    follows = streams & (place > 0)
    leads = streams & (place == 0)

    def at(turn_id, core_id):
        return dict(device_id=(turn_id, core_id), device_id_type=MESH)

    def ring_peers(size, stride):
        here = lax.rem(turn // stride, size)
        return [turn + (lax.rem(here + shift, size) - here) * stride for shift in range(1, size)]

    rings = [(size_y, 1), (size_z, size_y), (size_x, size_y * size_z)]

    own_copy = pltpu.make_async_copy(
        skew.at[core], skew_own.at[pl.ds(core * half, half)], local_sem.at[0]
    )
    own_copy.start()
    gain_copy = pltpu.make_async_copy(gain_cross, g_full, local_sem.at[1])
    gain_copy.start()
    smooth_copy = pltpu.make_async_copy(smooth_cross, m_full, local_sem.at[2])
    smooth_copy.start()

    barrier = pltpu.get_barrier_semaphore()
    count = 1
    pl.semaphore_signal(barrier, inc=1, **at(turn, other))
    for size, stride in rings:
        for peer in ring_peers(size, stride):
            pl.semaphore_signal(barrier, inc=1, **at(peer, core))
            count += 1

    @pl.when(turn > 0)
    def _():
        for target in range(2):
            pl.semaphore_signal(barrier, inc=1, **at(source, target))

    @pl.when(turn < turns - 1)
    def _():
        for target in range(2):
            pl.semaphore_signal(barrier, inc=1, **at(turn + 1, target))

    slot = turn * 2 + core
    sensor_ids = lax.broadcasted_iota(jnp.int32, sensor_step.shape, 0) * LANES
    sensor_ids += lax.broadcasted_iota(jnp.int32, sensor_step.shape, 1)
    found = jnp.where(sensor_ids == obs_sensor[0], sensor_step[...], 0).astype(F32)
    found = jnp.sum(jnp.sum(found, axis=0, keepdims=True), axis=1, keepdims=True)
    lane = lax.broadcasted_iota(jnp.int32, (1, LANES), 1)
    meta_row = jnp.where(
        lane == 0, obs_prec[0], jnp.where(lane == 1, found, obs_block[0].astype(F32))
    )
    obs[slot, 0:1, :] = obs_prec[0] * obs_values[...]
    obs[slot, 1:2, :] = meta_row
    ends = jnp.where(turn > 0, 2, 0) + jnp.where(sends_one, 2, 0)
    ends += jnp.where(sends_all, 2 * group, 0)
    pl.semaphore_wait(barrier, count + ends)

    skew_send = pltpu.make_async_remote_copy(
        src_ref=skew.at[other],
        dst_ref=skew_own.at[pl.ds(core * half, half)],
        send_sem=skew_sem.at[0],
        recv_sem=skew_sem.at[1],
        **at(turn, other),
    )
    skew_send.start()

    sent = []

    def obs_copy(first, rows, target, core_id, index):
        rows_ref = obs.at[pl.ds(first, rows)]
        copy = pltpu.make_async_remote_copy(
            src_ref=rows_ref,
            dst_ref=rows_ref,
            send_sem=obs_send.at[index],
            recv_sem=obs_recv.at[index],
            **at(target, core_id),
        )
        copy.start()
        sent.append(copy)
        return copy

    def obs_ring(number):
        size, stride = rings[number]
        rows = 2 * stride
        first = turn // stride * rows
        copies = []
        for index, peer in enumerate(ring_peers(size, stride)):
            copies.append(obs_copy(first, rows, peer, core, 1 + 3 * number + index))
        return copies

    core_copies = [obs_copy(slot, 1, turn, other, 0)]

    gain_copy.wait()

    def gain_turn(block, carry):
        rows = pl.ds(pl.multiple_of(block * LANES, LANES), LANES)
        value = g_full[rows, :] + eye_rows(block * LANES, LANES, width) * jnp.concatenate(
            [gain_diag[group : group + 1, :] for group in range(width // LANES)], axis=1
        )
        g_high[rows, :], g_low[rows, :] = split(value)
        return carry

    lax.fori_loop(0, width // LANES, gain_turn, 0)
    for copy in core_copies:
        copy.wait()
    ring_copies = obs_ring(0)
    own_copy.wait()
    skew_send.wait()

    def skew_turn(block, carry):
        rows = pl.ds(pl.multiple_of(block * LANES, LANES), LANES)
        value = STEP * (skew_own[rows, :].astype(F32) - skew_own[:, rows].astype(F32).T)
        a_high[rows, :], a_low[rows, :] = split(value)
        return carry

    lax.fori_loop(0, width // LANES, skew_turn, 0)

    strip = 256

    def square_turn(block, carry):
        rows = pl.ds(pl.multiple_of(block * strip, strip), strip)
        value = dot3(a_high[rows, :], a_low[rows, :], a_high[...], a_low[...])
        b_high[rows, :], b_low[rows, :] = split(value)
        a_value = a_high[rows, :].astype(F32) + a_low[rows, :].astype(F32)
        w_value = 0.5 * eye_rows(block * strip, strip, width) + a_value / 6.0 + value / 24.0
        w_high[rows, :], w_low[rows, :] = split(w_value)
        return carry

    lax.fori_loop(0, width // strip // 2, square_turn, 0)
    for copy in ring_copies:
        copy.wait()
    ring_copies = obs_ring(1)
    lax.fori_loop(width // strip // 2, width // strip, square_turn, 0)
    for copy in ring_copies:
        copy.wait()
    ring_copies = obs_ring(2)

    def tangent_turn(block, carry):
        rows = pl.ds(pl.multiple_of(block * strip, strip), strip)
        value = dot3(b_high[rows, :], b_low[rows, :], w_high[...], w_low[...])
        a_value = a_high[rows, :].astype(F32) + a_low[rows, :].astype(F32)
        value = eye_rows(block * strip, strip, width) + a_value + value
        tangent[rows, :] = value
        return carry

    lax.fori_loop(0, width // strip, tangent_turn, 0)
    for copy in ring_copies:
        copy.wait()

    meta = obs[:, 1, :].T
    weighted = obs[:, 0, :]
    block_ids = lax.broadcasted_iota(jnp.int32, (blocks, LANES), 0).astype(F32)
    for index in range(2):
        step = (turn * 2 + index).astype(F32)
        chosen = jnp.where((meta[1:2, :] == step) & (meta[2:3, :] == block_ids), 1.0, 0.0)
        weight = jnp.sum(chosen * meta[0:1, :], axis=1, keepdims=True)
        value = jnp.dot(chosen, weighted, precision=lax.Precision.HIGHEST, preferred_element_type=F32)
        share[index] = jnp.broadcast_to(weight / (weight + 1.0), (blocks, LANES))
        goal[index] = value / (weight + 1.0)
    for column in range(blocks):
        share_wide[:, column * LANES : (column + 1) * LANES] = share[core]

    def shared_turn(block, carry):
        rows = pl.ds(pl.multiple_of(block * LANES, LANES), LANES)
        value = tangent[rows, :] * share_wide[pl.ds(block, 1), :]
        w_high[rows, :], w_low[rows, :] = split(value)
        return carry

    lax.fori_loop(0, blocks, shared_turn, 0)

    def map_copy(block, part):
        ref = (p_high, p_low)[part]
        strip_ref = ref.at[core, pl.ds(pl.multiple_of(block * strip, strip), strip)]
        return pltpu.make_async_remote_copy(
            src_ref=strip_ref,
            dst_ref=strip_ref,
            send_sem=map_sem.at[0, part],
            recv_sem=map_sem.at[1, part],
            **at(turn, other),
        )

    def map_turn(block, carry):
        rows = pl.ds(pl.multiple_of(block * strip, strip), strip)

        @pl.when(block > 0)
        def _():
            map_copy(block - 1, 0).start()
            map_copy(block - 1, 1).start()

        value = tangent[rows, :] - dot3(g_high[rows, :], g_low[rows, :], w_high[...], w_low[...])
        p_high[core, rows, :], p_low[core, rows, :] = split(value)
        return carry

    lax.fori_loop(0, width // strip, map_turn, 0)

    gain_tile = square(g_full)
    matvec_loop(gain_tile, [goal[0], goal[1]], [gain_goal.at[0], gain_goal.at[1]], blocks, blocks)
    for index in range(2):
        gain_goal[index] += gain_diag[...] * goal[index]
    map_copy(width // strip - 1, 0).start()
    map_copy(width // strip - 1, 1).start()
    for part in range(2):
        ref = (p_high, p_low)[part]
        whole = pltpu.make_async_remote_copy(
            src_ref=ref.at[core],
            dst_ref=ref.at[other],
            send_sem=map_sem.at[0, part],
            recv_sem=map_sem.at[1, part],
            **at(turn, other),
        )
        whole.wait_send()
        whole.wait_recv()

    def eye_block(block):
        row = lax.broadcasted_iota(jnp.int32, (CHUNK, width), 0) + core * half + block * CHUNK
        return row == lax.broadcasted_iota(jnp.int32, (CHUNK, width), 1)

    def block_copies(block):
        return [
            pltpu.make_async_remote_copy(
                src_ref=out_ref.at[block],
                dst_ref=in_ref.at[block],
                send_sem=block_send.at[block, index],
                recv_sem=block_recv.at[block, index],
                **at(turn + 1, core),
            )
            for index, (out_ref, in_ref) in enumerate(
                ((coded_out, coded_in), (scales_out, scales_in))
            )
        ]

    def send_block(value, block):
        diagonal = eye_block(block)
        rest = jnp.where(diagonal, 0.0, value)
        largest = jnp.max(jnp.abs(rest), axis=0, keepdims=True)
        factor = jnp.where(largest > 1e-30, LEVELS / jnp.maximum(largest, 1e-30), 0.0)
        coded_out[block] = jnp.round(rest * factor).astype(jnp.int32).astype(jnp.int16)
        scales_out[block, 0:1, :] = largest * (1.0 / LEVELS)
        scales_out[block, 1:2, :] = jnp.sum(value - rest, axis=0, keepdims=True)
        for copy in block_copies(block):
            copy.start()

    def product(left_high, left_low, right_high, right_low):
        both = dot(left_high, jnp.concatenate([right_high, right_low], axis=1))
        return (both[:, LANES:] + dot(left_low, right_high)) + both[:, :LANES]

    def lane_block(start):
        return pl.ds(pl.multiple_of(start, LANES), LANES)

    def compose_turn(block, carry):
        columns = lane_block(core * half + block * LANES)
        value = product(p_high[1], p_low[1], p_high[0, :, columns], p_low[0, :, columns])
        composed[:, lane_block(block * LANES)] = value
        turned = value.T
        c_high[columns, :], c_low[columns, :] = split(turned)

        @pl.when(leads)
        def _():
            for index in range(LANES // CHUNK):
                chunk = turned[index * CHUNK : (index + 1) * CHUNK]
                send_block(chunk, block * (LANES // CHUNK) + index)

        return carry

    lax.fori_loop(0, 1, compose_turn, 0)
    matvec_loop(pair_tile(p_high.at[1], p_low.at[1]), [gain_goal[0]], [offset], blocks, blocks)
    offset[...] += gain_goal[1]
    offset_copy = pltpu.make_async_remote_copy(
        src_ref=offset,
        dst_ref=offset_in,
        send_sem=offset_sem.at[0],
        recv_sem=offset_sem.at[1],
        **at(turn + 1, core),
    )

    @pl.when(leads)
    def _():
        offset_copy.start()

    lax.fori_loop(1, parts, compose_turn, 0)
    own_rows = pl.ds(pl.multiple_of(core * half, half), half)
    whole_copies = [
        pltpu.make_async_remote_copy(
            src_ref=ref.at[own_rows],
            dst_ref=ref.at[own_rows],
            send_sem=whole_sem.at[0, index],
            recv_sem=whole_sem.at[1, index],
            **at(turn, other),
        )
        for index, ref in enumerate((c_high, c_low))
    ]

    @pl.when(follows)
    def _():
        for copy in whole_copies:
            copy.start()

    @pl.when(follows)
    def _():
        for copy in whole_copies:
            copy.wait()

        offset_copy.wait_recv()
        row = jnp.concatenate([offset_in[block : block + 1, :] for block in range(blocks)], axis=1)
        high = row.astype(BF16).astype(F32)
        empty = jnp.zeros((6, width), F32)
        left = jnp.concatenate([high, row - high, empty], axis=0).astype(BF16)
        both = dot(left, c_high[...])
        row = both[0:1] + (both[1:2] + dot(left, c_low[...])[0:1])
        for block in range(blocks):
            offset[block : block + 1, :] += row[:, block * LANES : (block + 1) * LANES]

        @pl.when(place < group - 1)
        def _():
            offset_copy.start()

        def stream_turn(lane_index, carry):
            columns = lane_block(lane_index * LANES)
            for index in range(LANES // CHUNK):
                block = lane_index * (LANES // CHUNK) + index
                for copy in block_copies(block):
                    copy.wait_recv()
                value = coded_in[block].astype(jnp.int32).astype(F32) * scales_in[block, 0:1, :]
                value += jnp.where(eye_block(block), scales_in[block, 1:2, :], 0.0)
                rows = pl.ds(index * CHUNK, CHUNK)
                turned_in[rows, :] = value
                high, low = split(value)
                both = dot(jnp.concatenate([high, low], axis=0), c_high[...])
                value = both[:CHUNK] + (both[CHUNK:] + dot(high, c_low[...]))

                @pl.when(place < group - 1)
                def _():
                    send_block(value, block)

                @pl.when(place == group - 1)
                def _():
                    turned_out[rows, :] = value

            prefix[:, columns] = turned_in[...].T

            @pl.when(place == group - 1)
            def _():
                composed[:, columns] = turned_out[...].T

            return carry

        lax.fori_loop(0, parts, stream_turn, 0)

    @pl.when(turn == 0)
    def _():
        state[...] = init[...]

    @pl.when(turn > 0)
    def _():
        pltpu.make_async_copy(arrived, arrived, chain_recv).wait()
        state[...] = arrived[0] + arrived[1]

    own_half = pl.ds(core * parts, parts)

    def chain_copies(count):
        order = [count - 1] + list(range(count - 1))
        return [
            pltpu.make_async_remote_copy(
                src_ref=outgoing,
                dst_ref=arrived.at[core],
                send_sem=chain_send.at[2 * step + target],
                recv_sem=chain_recv,
                **at(turn + 1 + step, target),
            )
            for step in order
            for target in range(2)
        ]

    @pl.when(sends_one | sends_all)
    def _():
        moved = matvec(square(composed), [state[own_half, :]], blocks, parts)[0]
        outgoing[...] = moved + jnp.where(core == 0, offset[...], 0.0)

    @pl.when(sends_one)
    def _():
        for copy in chain_copies(1):
            copy.start()

    @pl.when(sends_all)
    def _():
        for copy in chain_copies(group):
            copy.start()

    partial_copy = pltpu.make_async_remote_copy(
        src_ref=partial_out,
        dst_ref=partial_in,
        send_sem=partial_sem.at[0],
        recv_sem=partial_sem.at[1],
        **at(turn, other),
    )

    @pl.when(follows)
    def _():
        moved = matvec(square(prefix), [state[own_half, :]], blocks, parts)[0]
        partial_out[...] = moved + jnp.where(core == 0, offset_in[...], 0.0)
        partial_copy.start()
        partial_copy.wait()
        state[...] = partial_out[...] + partial_in[...]

    @pl.when(core == 1)
    def _():
        matvec_loop(pair_tile(p_high.at[0], p_low.at[0]), [state[...]], [work.at[0]], blocks, blocks)
        state[...] = work[0] + gain_goal[0]

    matvec_loop(square(tangent), [state[...]], [work.at[0]], blocks, blocks)
    missing = goal[core] - share[core] * work[0]
    matvec_loop(gain_tile, [missing], [work.at[1]], blocks, blocks)
    increment = work[1] + gain_diag[...] * missing
    result_own[0] = increment
    result_own[1] = work[0] + increment

    far_copy = pltpu.make_async_remote_copy(
        src_ref=result_own,
        dst_ref=result_far,
        send_sem=last_send.at[2],
        recv_sem=far_recv,
        **at(turn, other),
    )

    def later_copy(target):
        return pltpu.make_async_remote_copy(
            src_ref=result_own.at[0],
            dst_ref=later.at[core],
            send_sem=last_send.at[target],
            recv_sem=later_recv,
            **at(turn - 1, target),
        )

    @pl.when(turn > 0)
    def _():
        later_copy(0).start()
        later_copy(1).start()

    far_copy.start()

    @pl.when(turn == turns - 1)
    def _():
        later[...] = jnp.zeros_like(later)

    far_copy.wait()
    smooth_copy.wait()

    @pl.when(turn < turns - 1)
    def _():
        pltpu.make_async_copy(later, later, later_recv).wait()

    smooth_tile = square(m_full)
    matvec_loop(smooth_tile, [later[0], later[1]], [work.at[0], work.at[1]], blocks, blocks)
    second = jnp.where(core == 1, result_own[0], result_far[0])
    first_carried = second + work[0] + smooth_diag[...] * later[0]
    second_carried = later[0] + work[1] + smooth_diag[...] * later[1]
    work[0] = first_carried
    work[1] = second_carried
    part = pl.ds(core * (blocks // 2), blocks // 2)

    def half_tile(block, group):
        start = pl.multiple_of(core * half + block * LANES, LANES)
        return m_full[pl.ds(start, LANES), pl.ds(group * LANES, LANES)]

    matvec_loop(
        half_tile, [first_carried, second_carried], [summed.at[0], summed.at[1]], blocks // 2, blocks
    )
    diag_part = smooth_diag[part, :]
    for index in range(2):
        mean = jnp.where(core == index, result_own[1, part, :], result_far[1, part, :])
        late = mean + summed[index] + diag_part * work[index, part, :]
        for column in range(blocks // 2):
            columns = pl.ds(column * LANES, LANES)
            result[index : index + 1, columns] = mean[column : column + 1, :]
            result[index + 2 : index + 3, columns] = late[column : column + 1, :]

    @pl.when(leads | (follows & (place < group - 1)))
    def _():
        for block in range(chunks):
            for copy in block_copies(block):
                copy.wait_send()
        offset_copy.wait_send()

    @pl.when(sends_one)
    def _():
        for copy in chain_copies(1):
            copy.wait_send()

    @pl.when(sends_all)
    def _():
        for copy in chain_copies(group):
            copy.wait_send()

    @pl.when(turn > 0)
    def _():
        later_copy(0).wait_send()
        later_copy(1).wait_send()


def shards(
    dims,
    init_mean,
    jac_skew,
    gain_diag,
    gain_cross,
    smooth_diag,
    smooth_cross,
    obs_values,
    obs_prec,
    obs_sensor,
    obs_block,
    sensor_step,
):
    width = jac_skew.shape[2]
    blocks = width // LANES
    obs_total = lax.axis_size(("tm", "row"))
    vmem = pl.BlockSpec(memory_space=pltpu.VMEM)
    smem = pl.BlockSpec(memory_space=pltpu.SMEM)
    hbm = pl.BlockSpec(memory_space=pltpu.HBM)
    chunks = width // 2 // CHUNK
    group = dims[2]

    def wide(kind, lead=(), columns=width):
        return pltpu.VMEM(tuple(lead) + (width, columns), kind)

    def small(*lead):
        return pltpu.VMEM(tuple(lead) + (blocks, LANES), F32)

    dma = pltpu.SemaphoreType.DMA
    result = pl.pallas_call(
        functools.partial(kernel, dims),
        out_shape=jax.ShapeDtypeStruct((4, width // 2), F32),
        in_specs=[hbm, hbm, vmem, hbm, vmem, vmem, vmem, smem, smem, smem, vmem],
        out_specs=vmem,
        scratch_shapes=[
            wide(BF16),
            wide(BF16),
            wide(BF16),
            wide(BF16),
            wide(BF16),
            wide(BF16),
            wide(BF16),
            wide(F32),
            wide(F32),
            wide(BF16),
            wide(BF16),
            wide(F32),
            wide(BF16, (2,)),
            wide(BF16, (2,)),
            wide(F32, (), width // 2),
            wide(BF16),
            wide(BF16),
            wide(F32, (), width // 2),
            pltpu.VMEM((chunks, CHUNK, width), jnp.int16),
            pltpu.VMEM((chunks, CHUNK, width), jnp.int16),
            pltpu.VMEM((chunks, 2, width), F32),
            pltpu.VMEM((chunks, 2, width), F32),
            pltpu.VMEM((LANES, width), F32),
            pltpu.VMEM((LANES, width), F32),
            pltpu.VMEM((obs_total, 2, LANES), F32),
            pltpu.VMEM((blocks, width), F32),
            small(2),
            small(2),
            small(2),
            small(),
            small(),
            small(),
            small(),
            small(2),
            small(),
            small(),
            small(2),
            small(2),
            small(2),
            small(2),
            pltpu.VMEM((2, blocks // 2, LANES), F32),
            dma((3,)),
            dma((2,)),
            dma((2, 2)),
            dma((10,)),
            dma((10,)),
            dma((2, 2)),
            dma((chunks, 2)),
            dma((chunks, 2)),
            dma((2,)),
            dma((2,)),
            dma((2 * group,)),
            dma,
            dma((3,)),
            dma,
            dma,
        ],
        compiler_params=pltpu.CompilerParams(
            collective_id=0, has_side_effects=True, vmem_limit_bytes=VMEM_BYTES
        ),
    )(
        jac_skew,
        gain_cross,
        gain_diag.reshape(blocks, LANES),
        smooth_cross,
        smooth_diag.reshape(blocks, LANES),
        init_mean.reshape(blocks, LANES),
        obs_values,
        obs_prec,
        obs_sensor,
        obs_block,
        sensor_step.reshape(-1, LANES),
    )
    return result[:2], result[2:]


def solution(mesh):
    turns = mesh.shape["tm"]
    dims = {64: (4, 4, 4), 4: (1, 2, 2), 8: (2, 2, 2)}[turns]
    in_specs = (
        P(),
        P("tm", "row", None),
        P(),
        P(),
        P(),
        P(),
        P(("tm", "row"), None),
        P(("tm", "row")),
        P(("tm", "row")),
        P(("tm", "row")),
        P(),
    )
    out_specs = (P("tm", "row"), P("tm", "row"))
    return jax.shard_map(
        functools.partial(shards, dims),
        mesh=mesh,
        in_specs=in_specs,
        out_specs=out_specs,
        check_vma=False,
    )
```

```python
import functools

import jax
import jax.numpy as jnp
from jax import lax
from jax.experimental import pallas as pl
from jax.experimental.pallas import tpu as pltpu
from jax.sharding import PartitionSpec as P

F32 = jnp.float32
BF16 = jnp.bfloat16
MESH = pl.DeviceIdType.MESH
STEP = 0.25
LANES = 128
VMEM_BYTES = 67043328
LEVELS = 32767.0
CHUNK = 64
UNROLL = 4
dot = functools.partial(jnp.dot, preferred_element_type=F32)


def split(value):
    high = value.astype(BF16)
    return high, (value - high.astype(F32)).astype(BF16)


def dot3(left_high, left_low, right_high, right_low):
    return dot(left_high, right_low) + dot(left_low, right_high) + dot(left_high, right_high)


def eye_rows(first_row, rows, width):
    row = lax.broadcasted_iota(jnp.int32, (rows, width), 0) + first_row
    return (row == lax.broadcasted_iota(jnp.int32, (rows, width), 1)).astype(F32)


def matvec(tile, vectors, out_blocks, groups):
    rows = [[] for _ in vectors]
    for block in range(out_blocks):
        totals = [None] * len(vectors)
        for group in range(groups):
            entries = tile(block, group)
            for index, vector in enumerate(vectors):
                term = entries * vector[group : group + 1, :]
                totals[index] = term if totals[index] is None else totals[index] + term
        for index, total in enumerate(totals):
            rows[index].append(jnp.sum(total.T, axis=0, keepdims=True))
    return [jnp.concatenate(found, axis=0) for found in rows]


def matvec_loop(tile, vectors, outs, out_blocks, groups):
    def block_turn(turn, carry):
        first = turn * UNROLL
        found = matvec(lambda block, group: tile(first + block, group), vectors, UNROLL, groups)
        for index, rows in enumerate(found):
            for block in range(UNROLL):
                outs[index][pl.ds(first + block, 1), :] = rows[block : block + 1]
        return carry

    lax.fori_loop(0, out_blocks // UNROLL, block_turn, 0)


def square(ref):
    def tile(block, group):
        start = block * LANES if isinstance(block, int) else pl.multiple_of(block * LANES, LANES)
        return ref[pl.ds(start, LANES), pl.ds(group * LANES, LANES)]

    return tile


def pair_tile(high, low):
    def tile(block, group):
        where = (pl.ds(pl.multiple_of(block * LANES, LANES), LANES), pl.ds(group * LANES, LANES))
        return high[where].astype(F32) + low[where].astype(F32)

    return tile


def kernel(
    dims,
    skew,
    gain_cross,
    gain_diag,
    smooth_cross,
    smooth_diag,
    init,
    obs_values,
    obs_prec,
    obs_sensor,
    obs_block,
    sensor_step,
    result,
    skew_own,
    a_high,
    a_low,
    b_high,
    b_low,
    w_high,
    w_low,
    g_full,
    m_full,
    g_high,
    g_low,
    tangent,
    p_high,
    p_low,
    composed,
    c_high,
    c_low,
    prefix,
    coded_in,
    coded_out,
    scales_in,
    scales_out,
    turned_in,
    turned_out,
    obs,
    share_wide,
    share,
    goal,
    gain_goal,
    offset,
    offset_in,
    partial_out,
    partial_in,
    arrived,
    outgoing,
    state,
    work,
    result_own,
    result_far,
    later,
    summed,
    local_sem,
    skew_sem,
    map_sem,
    obs_send,
    obs_recv,
    whole_sem,
    block_send,
    block_recv,
    offset_sem,
    partial_sem,
    chain_send,
    chain_recv,
    last_send,
    far_recv,
    later_recv,
):
    turn = lax.axis_index("tm")
    core = lax.axis_index("row")
    turns = lax.axis_size("tm")
    width = gain_cross.shape[0]
    half = width // 2
    other = 1 - core
    size_x, size_z, size_y = dims
    blocks = width // LANES
    parts = half // LANES
    chunks = half // CHUNK
    group = size_y
    front = min(3, size_x * size_z - 1) * group
    place = lax.rem(turn, group)
    streams = turn >= front
    source = jnp.where(streams, turn - place, turn) - 1
    sends_one = turn < front - 1
    sends_all = (turn == front - 1) | (streams & (place == group - 1) & (turn < turns - 1))
    follows = streams & (place > 0)
    leads = streams & (place == 0)

    def at(turn_id, core_id):
        return dict(device_id=(turn_id, core_id), device_id_type=MESH)

    def ring_peers(size, stride):
        here = lax.rem(turn // stride, size)
        return [turn + (lax.rem(here + shift, size) - here) * stride for shift in range(1, size)]

    rings = [(size_y, 1), (size_z, size_y), (size_x, size_y * size_z)]

    own_copy = pltpu.make_async_copy(
        skew.at[core], skew_own.at[pl.ds(core * half, half)], local_sem.at[0]
    )
    own_copy.start()
    gain_copy = pltpu.make_async_copy(gain_cross, g_full, local_sem.at[1])
    gain_copy.start()
    smooth_copy = pltpu.make_async_copy(smooth_cross, m_full, local_sem.at[2])
    smooth_copy.start()

    barrier = pltpu.get_barrier_semaphore()
    count = 1
    pl.semaphore_signal(barrier, inc=1, **at(turn, other))
    for size, stride in rings:
        for peer in ring_peers(size, stride):
            pl.semaphore_signal(barrier, inc=1, **at(peer, core))
            count += 1

    @pl.when(turn > 0)
    def _():
        for target in range(2):
            pl.semaphore_signal(barrier, inc=1, **at(source, target))

    @pl.when(turn < turns - 1)
    def _():
        for target in range(2):
            pl.semaphore_signal(barrier, inc=1, **at(turn + 1, target))

    slot = turn * 2 + core
    sensor_ids = lax.broadcasted_iota(jnp.int32, sensor_step.shape, 0) * LANES
    sensor_ids += lax.broadcasted_iota(jnp.int32, sensor_step.shape, 1)
    found = jnp.where(sensor_ids == obs_sensor[...], sensor_step[...], 0).astype(F32)
    found = jnp.sum(jnp.sum(found, axis=0, keepdims=True), axis=1, keepdims=True)
    lane = lax.broadcasted_iota(jnp.int32, (1, LANES), 1)
    meta_row = jnp.where(
        lane == 0, obs_prec[...], jnp.where(lane == 1, found, obs_block[...].astype(F32))
    )
    obs[slot, 0:1, :] = obs_prec[...] * obs_values[...]
    obs[slot, 1:2, :] = meta_row
    ends = jnp.where(turn > 0, 2, 0) + jnp.where(sends_one, 2, 0)
    ends += jnp.where(sends_all, 2 * group, 0)
    pl.semaphore_wait(barrier, count + ends)

    skew_send = pltpu.make_async_remote_copy(
        src_ref=skew.at[other],
        dst_ref=skew_own.at[pl.ds(core * half, half)],
        send_sem=skew_sem.at[0],
        recv_sem=skew_sem.at[1],
        **at(turn, other),
    )
    skew_send.start()

    sent = []

    def obs_copy(first, rows, target, core_id, index):
        rows_ref = obs.at[pl.ds(first, rows)]
        copy = pltpu.make_async_remote_copy(
            src_ref=rows_ref,
            dst_ref=rows_ref,
            send_sem=obs_send.at[index],
            recv_sem=obs_recv.at[index],
            **at(target, core_id),
        )
        copy.start()
        sent.append(copy)
        return copy

    def obs_ring(number):
        size, stride = rings[number]
        rows = 2 * stride
        first = turn // stride * rows
        copies = []
        for index, peer in enumerate(ring_peers(size, stride)):
            copies.append(obs_copy(first, rows, peer, core, 1 + 3 * number + index))
        return copies

    core_copies = [obs_copy(slot, 1, turn, other, 0)]

    gain_copy.wait()

    def gain_turn(block, carry):
        rows = pl.ds(pl.multiple_of(block * LANES, LANES), LANES)
        value = g_full[rows, :] + eye_rows(block * LANES, LANES, width) * jnp.concatenate(
            [gain_diag[group : group + 1, :] for group in range(width // LANES)], axis=1
        )
        g_high[rows, :], g_low[rows, :] = split(value)
        return carry

    lax.fori_loop(0, width // LANES, gain_turn, 0)
    for copy in core_copies:
        copy.wait()
    ring_copies = obs_ring(0)
    own_copy.wait()
    skew_send.wait()

    def skew_turn(block, carry):
        rows = pl.ds(pl.multiple_of(block * LANES, LANES), LANES)
        value = STEP * (skew_own[rows, :].astype(F32) - skew_own[:, rows].astype(F32).T)
        a_high[rows, :], a_low[rows, :] = split(value)
        return carry

    lax.fori_loop(0, width // LANES, skew_turn, 0)

    strip = 256

    for block in range(width // strip):
        first = block * strip
        rows = slice(first, first + strip)
        value = dot3(a_high[rows, :], a_low[rows, :], a_high[:, first:], a_low[:, first:])
        tangent[rows, first:] = value
        if first:
            value = jnp.concatenate([tangent[:first, rows].T, value], axis=1)
        b_high[rows, :], b_low[rows, :] = split(value)
        a_value = a_high[rows, :].astype(F32) + a_low[rows, :].astype(F32)
        w_value = 0.5 * eye_rows(first, strip, width) + a_value / 6.0 + value / 24.0
        w_high[rows, :], w_low[rows, :] = split(w_value)
        if block % 2 == 1:
            for copy in ring_copies:
                copy.wait()
            ring_copies = obs_ring(1 + block // 2)

    def tangent_turn(block, carry):
        rows = pl.ds(pl.multiple_of(block * strip, strip), strip)
        value = dot3(b_high[rows, :], b_low[rows, :], w_high[...], w_low[...])
        a_value = a_high[rows, :].astype(F32) + a_low[rows, :].astype(F32)
        value = eye_rows(block * strip, strip, width) + a_value + value
        tangent[rows, :] = value
        return carry

    lax.fori_loop(0, width // strip, tangent_turn, 0)
    for copy in ring_copies:
        copy.wait()

    meta = obs[:, 1, :].T
    weighted = obs[:, 0, :]
    block_ids = lax.broadcasted_iota(jnp.int32, (blocks, LANES), 0).astype(F32)
    for index in range(2):
        step = (turn * 2 + index).astype(F32)
        chosen = jnp.where((meta[1:2, :] == step) & (meta[2:3, :] == block_ids), 1.0, 0.0)
        weight = jnp.sum(chosen * meta[0:1, :], axis=1, keepdims=True)
        value = jnp.dot(chosen, weighted, precision=lax.Precision.HIGHEST, preferred_element_type=F32)
        share[index] = jnp.broadcast_to(weight / (weight + 1.0), (blocks, LANES))
        goal[index] = value / (weight + 1.0)
    for column in range(blocks):
        share_wide[:, column * LANES : (column + 1) * LANES] = share[core]

    def shared_turn(block, carry):
        rows = pl.ds(pl.multiple_of(block * LANES, LANES), LANES)
        value = tangent[rows, :] * share_wide[pl.ds(block, 1), :]
        w_high[rows, :], w_low[rows, :] = split(value)
        return carry

    lax.fori_loop(0, blocks, shared_turn, 0)

    def map_copy(block, part):
        ref = (p_high, p_low)[part]
        strip_ref = ref.at[core, pl.ds(pl.multiple_of(block * strip, strip), strip)]
        return pltpu.make_async_remote_copy(
            src_ref=strip_ref,
            dst_ref=strip_ref,
            send_sem=map_sem.at[0, part],
            recv_sem=map_sem.at[1, part],
            **at(turn, other),
        )

    def map_turn(block, carry):
        rows = pl.ds(pl.multiple_of(block * strip, strip), strip)

        @pl.when(block > 0)
        def _():
            map_copy(block - 1, 0).start()
            map_copy(block - 1, 1).start()

        value = tangent[rows, :] - dot3(g_high[rows, :], g_low[rows, :], w_high[...], w_low[...])
        p_high[core, rows, :], p_low[core, rows, :] = split(value)
        return carry

    lax.fori_loop(0, width // strip, map_turn, 0)
    map_copy(width // strip - 1, 0).start()
    map_copy(width // strip - 1, 1).start()

    gain_tile = square(g_full)
    matvec_loop(gain_tile, [goal[0], goal[1]], [gain_goal.at[0], gain_goal.at[1]], blocks, blocks)
    for index in range(2):
        gain_goal[index] += gain_diag[...] * goal[index]
    for part in range(2):
        ref = (p_high, p_low)[part]
        whole = pltpu.make_async_remote_copy(
            src_ref=ref.at[core],
            dst_ref=ref.at[other],
            send_sem=map_sem.at[0, part],
            recv_sem=map_sem.at[1, part],
            **at(turn, other),
        )
        whole.wait_send()
        whole.wait_recv()

    def eye_block(block):
        row = lax.broadcasted_iota(jnp.int32, (CHUNK, width), 0) + core * half + block * CHUNK
        return row == lax.broadcasted_iota(jnp.int32, (CHUNK, width), 1)

    def block_copies(block):
        return [
            pltpu.make_async_remote_copy(
                src_ref=out_ref.at[block],
                dst_ref=in_ref.at[block],
                send_sem=block_send.at[block, index],
                recv_sem=block_recv.at[block, index],
                **at(turn + 1, core),
            )
            for index, (out_ref, in_ref) in enumerate(
                ((coded_out, coded_in), (scales_out, scales_in))
            )
        ]

    def send_block(value, block):
        diagonal = eye_block(block)
        rest = jnp.where(diagonal, 0.0, value)
        largest = jnp.max(jnp.abs(rest), axis=0, keepdims=True)
        factor = jnp.where(largest > 1e-30, LEVELS / jnp.maximum(largest, 1e-30), 0.0)
        coded_out[block] = jnp.round(rest * factor).astype(jnp.int32).astype(jnp.int16)
        scales_out[block, 0:1, :] = largest * (1.0 / LEVELS)
        scales_out[block, 1:2, :] = jnp.sum(value - rest, axis=0, keepdims=True)
        for copy in block_copies(block):
            copy.start()

    def product(left_high, left_low, right_high, right_low):
        both = dot(left_high, jnp.concatenate([right_high, right_low], axis=1))
        return (both[:, LANES:] + dot(left_low, right_high)) + both[:, :LANES]

    def lane_block(start):
        return pl.ds(pl.multiple_of(start, LANES), LANES)

    def compose_turn(block, carry):
        columns = lane_block(core * half + block * LANES)
        value = product(p_high[1], p_low[1], p_high[0, :, columns], p_low[0, :, columns])
        composed[:, lane_block(block * LANES)] = value
        turned = value.T
        c_high[columns, :], c_low[columns, :] = split(turned)

        @pl.when(leads)
        def _():
            for index in range(LANES // CHUNK):
                chunk = turned[index * CHUNK : (index + 1) * CHUNK]
                send_block(chunk, block * (LANES // CHUNK) + index)

        return carry

    lax.fori_loop(0, 1, compose_turn, 0)
    matvec_loop(pair_tile(p_high.at[1], p_low.at[1]), [gain_goal[0]], [offset], blocks, blocks)
    offset[...] += gain_goal[1]
    offset_copy = pltpu.make_async_remote_copy(
        src_ref=offset,
        dst_ref=offset_in,
        send_sem=offset_sem.at[0],
        recv_sem=offset_sem.at[1],
        **at(turn + 1, core),
    )

    @pl.when(leads)
    def _():
        offset_copy.start()

    lax.fori_loop(1, parts, compose_turn, 0)
    own_rows = pl.ds(pl.multiple_of(core * half, half), half)
    whole_copies = [
        pltpu.make_async_remote_copy(
            src_ref=ref.at[own_rows],
            dst_ref=ref.at[own_rows],
            send_sem=whole_sem.at[0, index],
            recv_sem=whole_sem.at[1, index],
            **at(turn, other),
        )
        for index, ref in enumerate((c_high, c_low))
    ]

    @pl.when(follows)
    def _():
        for copy in whole_copies:
            copy.start()

    @pl.when(follows)
    def _():
        for copy in whole_copies:
            copy.wait()

        offset_copy.wait_recv()
        row = jnp.concatenate([offset_in[block : block + 1, :] for block in range(blocks)], axis=1)
        high = row.astype(BF16).astype(F32)
        empty = jnp.zeros((6, width), F32)
        left = jnp.concatenate([high, row - high, empty], axis=0).astype(BF16)
        both = dot(left, c_high[...])
        row = both[0:1] + (both[1:2] + dot(left, c_low[...])[0:1])
        for block in range(blocks):
            offset[block : block + 1, :] += row[:, block * LANES : (block + 1) * LANES]

        @pl.when(place < group - 1)
        def _():
            offset_copy.start()

        def stream_turn(lane_index, carry):
            columns = lane_block(lane_index * LANES)
            for index in range(LANES // CHUNK):
                block = lane_index * (LANES // CHUNK) + index
                for copy in block_copies(block):
                    copy.wait_recv()
                value = coded_in[block].astype(jnp.int32).astype(F32) * scales_in[block, 0:1, :]
                value += jnp.where(eye_block(block), scales_in[block, 1:2, :], 0.0)
                rows = pl.ds(index * CHUNK, CHUNK)
                turned_in[rows, :] = value
                high, low = split(value)
                both = dot(jnp.concatenate([high, low], axis=0), c_high[...])
                value = both[:CHUNK] + (both[CHUNK:] + dot(high, c_low[...]))

                @pl.when(place < group - 1)
                def _():
                    send_block(value, block)

                @pl.when(place == group - 1)
                def _():
                    turned_out[rows, :] = value

            prefix[:, columns] = turned_in[...].T

            @pl.when(place == group - 1)
            def _():
                composed[:, columns] = turned_out[...].T

            return carry

        lax.fori_loop(0, parts, stream_turn, 0)

    @pl.when(turn == 0)
    def _():
        state[...] = init[...]

    @pl.when(turn > 0)
    def _():
        pltpu.make_async_copy(arrived, arrived, chain_recv).wait()
        state[...] = arrived[0] + arrived[1]

    own_half = pl.ds(core * parts, parts)

    def chain_copies(count):
        order = [count - 1] + list(range(count - 1))
        return [
            pltpu.make_async_remote_copy(
                src_ref=outgoing,
                dst_ref=arrived.at[core],
                send_sem=chain_send.at[2 * step + target],
                recv_sem=chain_recv,
                **at(turn + 1 + step, target),
            )
            for step in order
            for target in range(2)
        ]

    @pl.when(sends_one | sends_all)
    def _():
        moved = matvec(square(composed), [state[own_half, :]], blocks, parts)[0]
        outgoing[...] = moved + jnp.where(core == 0, offset[...], 0.0)

    @pl.when(sends_one)
    def _():
        for copy in chain_copies(1):
            copy.start()

    @pl.when(sends_all)
    def _():
        for copy in chain_copies(group):
            copy.start()

    partial_copy = pltpu.make_async_remote_copy(
        src_ref=partial_out,
        dst_ref=partial_in,
        send_sem=partial_sem.at[0],
        recv_sem=partial_sem.at[1],
        **at(turn, other),
    )

    @pl.when(follows)
    def _():
        moved = matvec(square(prefix), [state[own_half, :]], blocks, parts)[0]
        partial_out[...] = moved + jnp.where(core == 0, offset_in[...], 0.0)
        partial_copy.start()
        partial_copy.wait()
        state[...] = partial_out[...] + partial_in[...]

    @pl.when(core == 1)
    def _():
        matvec_loop(pair_tile(p_high.at[0], p_low.at[0]), [state[...]], [work.at[0]], blocks, blocks)
        state[...] = work[0] + gain_goal[0]

    matvec_loop(square(tangent), [state[...]], [work.at[0]], blocks, blocks)
    missing = goal[core] - share[core] * work[0]
    matvec_loop(gain_tile, [missing], [work.at[1]], blocks, blocks)
    increment = work[1] + gain_diag[...] * missing
    result_own[0] = increment
    result_own[1] = work[0] + increment

    far_copy = pltpu.make_async_remote_copy(
        src_ref=result_own,
        dst_ref=result_far,
        send_sem=last_send.at[2],
        recv_sem=far_recv,
        **at(turn, other),
    )

    def later_copy(target):
        return pltpu.make_async_remote_copy(
            src_ref=result_own.at[0],
            dst_ref=later.at[core],
            send_sem=last_send.at[target],
            recv_sem=later_recv,
            **at(turn - 1, target),
        )

    @pl.when(turn > 0)
    def _():
        later_copy(0).start()
        later_copy(1).start()

    far_copy.start()

    @pl.when(turn == turns - 1)
    def _():
        later[...] = jnp.zeros_like(later)

    far_copy.wait()
    smooth_copy.wait()

    @pl.when(turn < turns - 1)
    def _():
        pltpu.make_async_copy(later, later, later_recv).wait()

    smooth_tile = square(m_full)
    matvec_loop(smooth_tile, [later[0], later[1]], [work.at[0], work.at[1]], blocks, blocks)
    second = jnp.where(core == 1, result_own[0], result_far[0])
    first_carried = second + work[0] + smooth_diag[...] * later[0]
    second_carried = later[0] + work[1] + smooth_diag[...] * later[1]
    work[0] = first_carried
    work[1] = second_carried
    part = pl.ds(core * (blocks // 2), blocks // 2)

    def half_tile(block, group):
        start = pl.multiple_of(core * half + block * LANES, LANES)
        return m_full[pl.ds(start, LANES), pl.ds(group * LANES, LANES)]

    matvec_loop(
        half_tile, [first_carried, second_carried], [summed.at[0], summed.at[1]], blocks // 2, blocks
    )
    diag_part = smooth_diag[part, :]
    for index in range(2):
        mean = jnp.where(core == index, result_own[1, part, :], result_far[1, part, :])
        late = mean + summed[index] + diag_part * work[index, part, :]
        for column in range(blocks // 2):
            columns = pl.ds(column * LANES, LANES)
            result[index : index + 1, columns] = mean[column : column + 1, :]
            result[index + 2 : index + 3, columns] = late[column : column + 1, :]

    @pl.when(leads | (follows & (place < group - 1)))
    def _():
        for block in range(chunks):
            for copy in block_copies(block):
                copy.wait_send()
        offset_copy.wait_send()

    @pl.when(sends_one)
    def _():
        for copy in chain_copies(1):
            copy.wait_send()

    @pl.when(sends_all)
    def _():
        for copy in chain_copies(group):
            copy.wait_send()

    @pl.when(turn > 0)
    def _():
        later_copy(0).wait_send()
        later_copy(1).wait_send()


def shards(
    dims,
    init_mean,
    jac_skew,
    gain_diag,
    gain_cross,
    smooth_diag,
    smooth_cross,
    obs_values,
    obs_prec,
    obs_sensor,
    obs_block,
    sensor_step,
):
    width = jac_skew.shape[2]
    blocks = width // LANES
    obs_total = lax.axis_size(("tm", "row"))
    vmem = pl.BlockSpec(memory_space=pltpu.VMEM)
    hbm = pl.BlockSpec(memory_space=pltpu.HBM)
    chunks = width // 2 // CHUNK
    group = dims[2]

    def wide(kind, lead=(), columns=width):
        return pltpu.VMEM(tuple(lead) + (width, columns), kind)

    def small(*lead):
        return pltpu.VMEM(tuple(lead) + (blocks, LANES), F32)

    dma = pltpu.SemaphoreType.DMA
    result = pl.pallas_call(
        functools.partial(kernel, dims),
        out_shape=jax.ShapeDtypeStruct((4, width // 2), F32),
        in_specs=[hbm, hbm, vmem, hbm] + [vmem] * 7,
        out_specs=vmem,
        scratch_shapes=[
            wide(BF16),
            wide(BF16),
            wide(BF16),
            wide(BF16),
            wide(BF16),
            wide(BF16),
            wide(BF16),
            wide(F32),
            wide(F32),
            wide(BF16),
            wide(BF16),
            wide(F32),
            wide(BF16, (2,)),
            wide(BF16, (2,)),
            wide(F32, (), width // 2),
            wide(BF16),
            wide(BF16),
            wide(F32, (), width // 2),
            pltpu.VMEM((chunks, CHUNK, width), jnp.int16),
            pltpu.VMEM((chunks, CHUNK, width), jnp.int16),
            pltpu.VMEM((chunks, 2, width), F32),
            pltpu.VMEM((chunks, 2, width), F32),
            pltpu.VMEM((LANES, width), F32),
            pltpu.VMEM((LANES, width), F32),
            pltpu.VMEM((obs_total, 2, LANES), F32),
            pltpu.VMEM((blocks, width), F32),
            small(2),
            small(2),
            small(2),
            small(),
            small(),
            small(),
            small(),
            small(2),
            small(),
            small(),
            small(2),
            small(2),
            small(2),
            small(2),
            pltpu.VMEM((2, blocks // 2, LANES), F32),
            dma((3,)),
            dma((2,)),
            dma((2, 2)),
            dma((10,)),
            dma((10,)),
            dma((2, 2)),
            dma((chunks, 2)),
            dma((chunks, 2)),
            dma((2,)),
            dma((2,)),
            dma((2 * group,)),
            dma,
            dma((3,)),
            dma,
            dma,
        ],
        compiler_params=pltpu.CompilerParams(
            collective_id=0, has_side_effects=True, vmem_limit_bytes=VMEM_BYTES
        ),
    )(
        jac_skew,
        gain_cross,
        gain_diag.reshape(blocks, LANES),
        smooth_cross,
        smooth_diag.reshape(blocks, LANES),
        init_mean.reshape(blocks, LANES),
        obs_values,
        obs_prec.reshape(1, 1),
        obs_sensor.reshape(1, 1),
        obs_block.reshape(1, 1),
        sensor_step.reshape(-1, LANES),
    )
    return result[:2], result[2:]


def solution(mesh):
    turns = mesh.shape["tm"]
    dims = {64: (4, 4, 4), 4: (1, 2, 2), 8: (2, 2, 2)}[turns]
    in_specs = (
        P(),
        P("tm", "row", None),
        P(),
        P(),
        P(),
        P(),
        P(("tm", "row"), None),
        P(("tm", "row")),
        P(("tm", "row")),
        P(("tm", "row")),
        P(),
    )
    out_specs = (P("tm", "row"), P("tm", "row"))
    return jax.shard_map(
        functools.partial(shards, dims),
        mesh=mesh,
        in_specs=in_specs,
        out_specs=out_specs,
        check_vma=False,
    )
```

```python
import functools

import jax
import jax.numpy as jnp
from jax import lax
from jax.experimental import pallas as pl
from jax.experimental.pallas import tpu as pltpu
from jax.sharding import PartitionSpec as P

F32 = jnp.float32
BF16 = jnp.bfloat16
MESH = pl.DeviceIdType.MESH
STEP = 0.25
LANES = 128
VMEM_BYTES = 67043328
LEVELS = 32767.0
CHUNK = 64
UNROLL = 8
dot = functools.partial(jnp.dot, preferred_element_type=F32)


def split(value):
    high = value.astype(BF16)
    return high, (value - high.astype(F32)).astype(BF16)


def dot3(left_high, left_low, right_high, right_low):
    return dot(left_high, right_low) + dot(left_low, right_high) + dot(left_high, right_high)


def eye_rows(first_row, rows, width):
    row = lax.broadcasted_iota(jnp.int32, (rows, width), 0) + first_row
    return (row == lax.broadcasted_iota(jnp.int32, (rows, width), 1)).astype(F32)


def matvec(tile, vectors, out_blocks, groups):
    rows = [[] for _ in vectors]
    for block in range(out_blocks):
        totals = [None] * len(vectors)
        for group in range(groups):
            entries = tile(block, group)
            for index, vector in enumerate(vectors):
                term = entries * vector[group : group + 1, :]
                totals[index] = term if totals[index] is None else totals[index] + term
        for index, total in enumerate(totals):
            rows[index].append(jnp.sum(total.T, axis=0, keepdims=True))
    return [jnp.concatenate(found, axis=0) for found in rows]


def matvec_loop(tile, vectors, outs, out_blocks, groups):
    unroll = min(UNROLL, out_blocks)

    def block_turn(turn, carry):
        first = turn * unroll
        found = matvec(lambda block, group: tile(first + block, group), vectors, unroll, groups)
        for index, rows in enumerate(found):
            for block in range(unroll):
                outs[index][pl.ds(first + block, 1), :] = rows[block : block + 1]
        return carry

    lax.fori_loop(0, out_blocks // unroll, block_turn, 0)


def square(ref):
    def tile(block, group):
        start = block * LANES if isinstance(block, int) else pl.multiple_of(block * LANES, LANES)
        return ref[pl.ds(start, LANES), pl.ds(group * LANES, LANES)]

    return tile


def pair_tile(high, low):
    def tile(block, group):
        where = (pl.ds(pl.multiple_of(block * LANES, LANES), LANES), pl.ds(group * LANES, LANES))
        return high[where].astype(F32) + low[where].astype(F32)

    return tile


def kernel(
    dims,
    skew,
    gain_cross,
    gain_diag,
    smooth_cross,
    smooth_diag,
    init,
    obs_values,
    obs_prec,
    obs_sensor,
    obs_block,
    sensor_step,
    result,
    skew_own,
    a_high,
    a_low,
    b_high,
    b_low,
    w_high,
    w_low,
    g_full,
    m_full,
    g_high,
    g_low,
    tangent,
    p_high,
    p_low,
    composed,
    c_high,
    c_low,
    prefix,
    coded_in,
    coded_out,
    scales_in,
    scales_out,
    turned_in,
    turned_out,
    obs,
    share_wide,
    share,
    goal,
    gain_goal,
    offset,
    offset_in,
    partial_out,
    partial_in,
    arrived,
    outgoing,
    state,
    work,
    result_own,
    result_far,
    later,
    summed,
    local_sem,
    skew_sem,
    map_sem,
    obs_send,
    obs_recv,
    whole_sem,
    block_send,
    block_recv,
    offset_sem,
    partial_sem,
    chain_send,
    chain_recv,
    last_send,
    far_recv,
    later_recv,
):
    turn = lax.axis_index("tm")
    core = lax.axis_index("row")
    turns = lax.axis_size("tm")
    width = gain_cross.shape[0]
    half = width // 2
    other = 1 - core
    size_x, size_z, size_y = dims
    blocks = width // LANES
    parts = half // LANES
    chunks = half // CHUNK
    group = size_y
    front = min(3, size_x * size_z - 1) * group
    place = lax.rem(turn, group)
    streams = turn >= front
    source = jnp.where(streams, turn - place, turn) - 1
    sends_one = turn < front - 1
    sends_all = (turn == front - 1) | (streams & (place == group - 1) & (turn < turns - 1))
    follows = streams & (place > 0)
    leads = streams & (place == 0)

    def at(turn_id, core_id):
        return dict(device_id=(turn_id, core_id), device_id_type=MESH)

    def ring_peers(size, stride):
        here = lax.rem(turn // stride, size)
        return [turn + (lax.rem(here + shift, size) - here) * stride for shift in range(1, size)]

    rings = [(size_y, 1), (size_z, size_y), (size_x, size_y * size_z)]

    own_copy = pltpu.make_async_copy(
        skew.at[core], skew_own.at[pl.ds(core * half, half)], local_sem.at[0]
    )
    own_copy.start()
    gain_copy = pltpu.make_async_copy(gain_cross, g_full, local_sem.at[1])
    gain_copy.start()
    smooth_copy = pltpu.make_async_copy(smooth_cross, m_full, local_sem.at[2])
    smooth_copy.start()

    barrier = pltpu.get_barrier_semaphore()
    count = 1
    pl.semaphore_signal(barrier, inc=1, **at(turn, other))
    for size, stride in rings:
        for peer in ring_peers(size, stride):
            pl.semaphore_signal(barrier, inc=1, **at(peer, core))
            count += 1

    @pl.when(turn > 0)
    def _():
        for target in range(2):
            pl.semaphore_signal(barrier, inc=1, **at(source, target))

    @pl.when(turn < turns - 1)
    def _():
        for target in range(2):
            pl.semaphore_signal(barrier, inc=1, **at(turn + 1, target))

    slot = turn * 2 + core
    sensor_ids = lax.broadcasted_iota(jnp.int32, sensor_step.shape, 0) * LANES
    sensor_ids += lax.broadcasted_iota(jnp.int32, sensor_step.shape, 1)
    found = jnp.where(sensor_ids == obs_sensor[...], sensor_step[...], 0).astype(F32)
    found = jnp.sum(jnp.sum(found, axis=0, keepdims=True), axis=1, keepdims=True)
    lane = lax.broadcasted_iota(jnp.int32, (1, LANES), 1)
    meta_row = jnp.where(
        lane == 0, obs_prec[...], jnp.where(lane == 1, found, obs_block[...].astype(F32))
    )
    obs[slot, 0:1, :] = obs_prec[...] * obs_values[...]
    obs[slot, 1:2, :] = meta_row
    ends = jnp.where(turn > 0, 2, 0) + jnp.where(sends_one, 2, 0)
    ends += jnp.where(sends_all, 2 * group, 0)
    pl.semaphore_wait(barrier, count + ends)

    skew_send = pltpu.make_async_remote_copy(
        src_ref=skew.at[other],
        dst_ref=skew_own.at[pl.ds(core * half, half)],
        send_sem=skew_sem.at[0],
        recv_sem=skew_sem.at[1],
        **at(turn, other),
    )
    skew_send.start()

    sent = []

    def obs_copy(first, rows, target, core_id, index):
        rows_ref = obs.at[pl.ds(first, rows)]
        copy = pltpu.make_async_remote_copy(
            src_ref=rows_ref,
            dst_ref=rows_ref,
            send_sem=obs_send.at[index],
            recv_sem=obs_recv.at[index],
            **at(target, core_id),
        )
        copy.start()
        sent.append(copy)
        return copy

    def obs_ring(number):
        size, stride = rings[number]
        rows = 2 * stride
        first = turn // stride * rows
        copies = []
        for index, peer in enumerate(ring_peers(size, stride)):
            copies.append(obs_copy(first, rows, peer, core, 1 + 3 * number + index))
        return copies

    core_copies = [obs_copy(slot, 1, turn, other, 0)]

    gain_copy.wait()

    def gain_turn(block, carry):
        rows = pl.ds(pl.multiple_of(block * LANES, LANES), LANES)
        value = g_full[rows, :] + eye_rows(block * LANES, LANES, width) * jnp.concatenate(
            [gain_diag[group : group + 1, :] for group in range(width // LANES)], axis=1
        )
        g_high[rows, :], g_low[rows, :] = split(value)
        return carry

    lax.fori_loop(0, width // LANES, gain_turn, 0)
    for copy in core_copies:
        copy.wait()
    ring_copies = obs_ring(0)
    own_copy.wait()
    skew_send.wait()

    def skew_turn(block, carry):
        rows = pl.ds(pl.multiple_of(block * LANES, LANES), LANES)
        value = STEP * (skew_own[rows, :].astype(F32) - skew_own[:, rows].astype(F32).T)
        a_high[rows, :], a_low[rows, :] = split(value)
        return carry

    lax.fori_loop(0, width // LANES, skew_turn, 0)

    strip = 256

    for block in range(width // strip):
        first = block * strip
        rows = slice(first, first + strip)
        value = dot3(a_high[rows, :], a_low[rows, :], a_high[:, first:], a_low[:, first:])
        tangent[rows, first:] = value
        if first:
            value = jnp.concatenate([tangent[:first, rows].T, value], axis=1)
        b_high[rows, :], b_low[rows, :] = split(value)
        a_value = a_high[rows, :].astype(F32) + a_low[rows, :].astype(F32)
        w_value = 0.5 * eye_rows(first, strip, width) + a_value / 6.0 + value / 24.0
        w_high[rows, :], w_low[rows, :] = split(w_value)
        if block % 2 == 1:
            for copy in ring_copies:
                copy.wait()
            ring_copies = obs_ring(1 + block // 2)

    broad = 512

    def tangent_turn(block, carry):
        rows = pl.ds(pl.multiple_of(block * broad, broad), broad)
        value = dot3(b_high[rows, :], b_low[rows, :], w_high[...], w_low[...])
        a_value = a_high[rows, :].astype(F32) + a_low[rows, :].astype(F32)
        value = eye_rows(block * broad, broad, width) + a_value + value
        tangent[rows, :] = value
        return carry

    lax.fori_loop(0, width // broad, tangent_turn, 0)
    for copy in ring_copies:
        copy.wait()

    meta = obs[:, 1, :].T
    weighted = obs[:, 0, :]
    block_ids = lax.broadcasted_iota(jnp.int32, (blocks, LANES), 0).astype(F32)
    for index in range(2):
        step = (turn * 2 + index).astype(F32)
        chosen = jnp.where((meta[1:2, :] == step) & (meta[2:3, :] == block_ids), 1.0, 0.0)
        weight = jnp.sum(chosen * meta[0:1, :], axis=1, keepdims=True)
        value = jnp.dot(chosen, weighted, precision=lax.Precision.HIGHEST, preferred_element_type=F32)
        share[index] = jnp.broadcast_to(weight / (weight + 1.0), (blocks, LANES))
        goal[index] = value / (weight + 1.0)
    for column in range(blocks):
        share_wide[:, column * LANES : (column + 1) * LANES] = share[core]

    def shared_turn(block, carry):
        rows = pl.ds(pl.multiple_of(block * LANES, LANES), LANES)
        value = tangent[rows, :] * share_wide[pl.ds(block, 1), :]
        w_high[rows, :], w_low[rows, :] = split(value)
        return carry

    lax.fori_loop(0, blocks, shared_turn, 0)

    def map_copy(block, part):
        ref = (p_high, p_low)[part]
        strip_ref = ref.at[core, pl.ds(pl.multiple_of(block * strip, strip), strip)]
        return pltpu.make_async_remote_copy(
            src_ref=strip_ref,
            dst_ref=strip_ref,
            send_sem=map_sem.at[0, part],
            recv_sem=map_sem.at[1, part],
            **at(turn, other),
        )

    def map_turn(block, carry):
        rows = pl.ds(pl.multiple_of(block * strip, strip), strip)

        @pl.when(block > 0)
        def _():
            map_copy(block - 1, 0).start()
            map_copy(block - 1, 1).start()

        value = tangent[rows, :] - dot3(g_high[rows, :], g_low[rows, :], w_high[...], w_low[...])
        p_high[core, rows, :], p_low[core, rows, :] = split(value)
        return carry

    lax.fori_loop(0, width // strip, map_turn, 0)
    map_copy(width // strip - 1, 0).start()
    map_copy(width // strip - 1, 1).start()

    gain_tile = square(g_full)
    matvec_loop(gain_tile, [goal[0], goal[1]], [gain_goal.at[0], gain_goal.at[1]], blocks, blocks)
    for index in range(2):
        gain_goal[index] += gain_diag[...] * goal[index]
    for part in range(2):
        ref = (p_high, p_low)[part]
        whole = pltpu.make_async_remote_copy(
            src_ref=ref.at[core],
            dst_ref=ref.at[other],
            send_sem=map_sem.at[0, part],
            recv_sem=map_sem.at[1, part],
            **at(turn, other),
        )
        whole.wait_send()
        whole.wait_recv()

    def eye_block(block):
        row = lax.broadcasted_iota(jnp.int32, (CHUNK, width), 0) + core * half + block * CHUNK
        return row == lax.broadcasted_iota(jnp.int32, (CHUNK, width), 1)

    def block_copies(block):
        return [
            pltpu.make_async_remote_copy(
                src_ref=out_ref.at[block],
                dst_ref=in_ref.at[block],
                send_sem=block_send.at[block, index],
                recv_sem=block_recv.at[block, index],
                **at(turn + 1, core),
            )
            for index, (out_ref, in_ref) in enumerate(
                ((coded_out, coded_in), (scales_out, scales_in))
            )
        ]

    def send_block(value, block):
        diagonal = eye_block(block)
        rest = jnp.where(diagonal, 0.0, value)
        largest = jnp.max(jnp.abs(rest), axis=0, keepdims=True)
        factor = jnp.where(largest > 1e-30, LEVELS / jnp.maximum(largest, 1e-30), 0.0)
        coded_out[block] = jnp.round(rest * factor).astype(jnp.int32).astype(jnp.int16)
        scales_out[block, 0:1, :] = largest * (1.0 / LEVELS)
        scales_out[block, 1:2, :] = jnp.sum(value - rest, axis=0, keepdims=True)
        for copy in block_copies(block):
            copy.start()

    def product(left_high, left_low, right_high, right_low):
        both = dot(left_high, jnp.concatenate([right_high, right_low], axis=1))
        return (both[:, LANES:] + dot(left_low, right_high)) + both[:, :LANES]

    def lane_block(start):
        return pl.ds(pl.multiple_of(start, LANES), LANES)

    def compose_turn(block, carry):
        columns = lane_block(core * half + block * LANES)
        value = product(p_high[1], p_low[1], p_high[0, :, columns], p_low[0, :, columns])
        composed[:, lane_block(block * LANES)] = value
        turned = value.T
        c_high[columns, :], c_low[columns, :] = split(turned)

        @pl.when(leads)
        def _():
            for index in range(LANES // CHUNK):
                chunk = turned[index * CHUNK : (index + 1) * CHUNK]
                send_block(chunk, block * (LANES // CHUNK) + index)

        return carry

    lax.fori_loop(0, 1, compose_turn, 0)
    matvec_loop(pair_tile(p_high.at[1], p_low.at[1]), [gain_goal[0]], [offset], blocks, blocks)
    offset[...] += gain_goal[1]
    offset_copy = pltpu.make_async_remote_copy(
        src_ref=offset,
        dst_ref=offset_in,
        send_sem=offset_sem.at[0],
        recv_sem=offset_sem.at[1],
        **at(turn + 1, core),
    )

    @pl.when(leads)
    def _():
        offset_copy.start()

    lax.fori_loop(1, parts, compose_turn, 0)
    own_rows = pl.ds(pl.multiple_of(core * half, half), half)
    whole_copies = [
        pltpu.make_async_remote_copy(
            src_ref=ref.at[own_rows],
            dst_ref=ref.at[own_rows],
            send_sem=whole_sem.at[0, index],
            recv_sem=whole_sem.at[1, index],
            **at(turn, other),
        )
        for index, ref in enumerate((c_high, c_low))
    ]

    @pl.when(follows)
    def _():
        for copy in whole_copies:
            copy.start()

    @pl.when(follows)
    def _():
        for copy in whole_copies:
            copy.wait()

        offset_copy.wait_recv()
        row = jnp.concatenate([offset_in[block : block + 1, :] for block in range(blocks)], axis=1)
        high = row.astype(BF16).astype(F32)
        empty = jnp.zeros((6, width), F32)
        left = jnp.concatenate([high, row - high, empty], axis=0).astype(BF16)
        both = dot(left, c_high[...])
        row = both[0:1] + (both[1:2] + dot(left, c_low[...])[0:1])
        for block in range(blocks):
            offset[block : block + 1, :] += row[:, block * LANES : (block + 1) * LANES]

        @pl.when(place < group - 1)
        def _():
            offset_copy.start()

        def stream_turn(lane_index, carry):
            columns = lane_block(lane_index * LANES)
            for index in range(LANES // CHUNK):
                block = lane_index * (LANES // CHUNK) + index
                for copy in block_copies(block):
                    copy.wait_recv()
                value = coded_in[block].astype(jnp.int32).astype(F32) * scales_in[block, 0:1, :]
                value += jnp.where(eye_block(block), scales_in[block, 1:2, :], 0.0)
                rows = pl.ds(index * CHUNK, CHUNK)
                turned_in[rows, :] = value
                high, low = split(value)
                both = dot(jnp.concatenate([high, low], axis=0), c_high[...])
                value = both[:CHUNK] + (both[CHUNK:] + dot(high, c_low[...]))

                @pl.when(place < group - 1)
                def _():
                    send_block(value, block)

                @pl.when(place == group - 1)
                def _():
                    turned_out[rows, :] = value

            prefix[:, columns] = turned_in[...].T

            @pl.when(place == group - 1)
            def _():
                composed[:, columns] = turned_out[...].T

            return carry

        lax.fori_loop(0, parts, stream_turn, 0)

    @pl.when(turn == 0)
    def _():
        state[...] = init[...]

    @pl.when(turn > 0)
    def _():
        pltpu.make_async_copy(arrived, arrived, chain_recv).wait()
        state[...] = arrived[0] + arrived[1]

    own_half = pl.ds(core * parts, parts)

    def chain_copies(count):
        order = [count - 1] + list(range(count - 1))
        return [
            pltpu.make_async_remote_copy(
                src_ref=outgoing,
                dst_ref=arrived.at[core],
                send_sem=chain_send.at[2 * step + target],
                recv_sem=chain_recv,
                **at(turn + 1 + step, lax.rem(core + target, 2)),
            )
            for step in order
            for target in range(2)
        ]

    @pl.when(sends_one | sends_all)
    def _():
        moved = matvec(square(composed), [state[own_half, :]], blocks, parts)[0]
        outgoing[...] = moved + jnp.where(core == 0, offset[...], 0.0)

    @pl.when(sends_one)
    def _():
        for copy in chain_copies(1):
            copy.start()

    @pl.when(sends_all)
    def _():
        for copy in chain_copies(group):
            copy.start()

    partial_copy = pltpu.make_async_remote_copy(
        src_ref=partial_out,
        dst_ref=partial_in,
        send_sem=partial_sem.at[0],
        recv_sem=partial_sem.at[1],
        **at(turn, other),
    )

    @pl.when(follows)
    def _():
        moved = matvec(square(prefix), [state[own_half, :]], blocks, parts)[0]
        partial_out[...] = moved + jnp.where(core == 0, offset_in[...], 0.0)
        partial_copy.start()
        partial_copy.wait()
        state[...] = partial_out[...] + partial_in[...]

    @pl.when(core == 1)
    def _():
        matvec_loop(pair_tile(p_high.at[0], p_low.at[0]), [state[...]], [work.at[0]], blocks, blocks)
        state[...] = work[0] + gain_goal[0]

    matvec_loop(square(tangent), [state[...]], [work.at[0]], blocks, blocks)
    missing = goal[core] - share[core] * work[0]
    matvec_loop(gain_tile, [missing], [work.at[1]], blocks, blocks)
    increment = work[1] + gain_diag[...] * missing
    result_own[0] = increment
    result_own[1] = work[0] + increment

    far_copy = pltpu.make_async_remote_copy(
        src_ref=result_own,
        dst_ref=result_far,
        send_sem=last_send.at[2],
        recv_sem=far_recv,
        **at(turn, other),
    )

    def later_copy(target):
        return pltpu.make_async_remote_copy(
            src_ref=result_own.at[0],
            dst_ref=later.at[core],
            send_sem=last_send.at[target],
            recv_sem=later_recv,
            **at(turn - 1, target),
        )

    @pl.when(turn > 0)
    def _():
        later_copy(0).start()
        later_copy(1).start()

    far_copy.start()

    @pl.when(turn == turns - 1)
    def _():
        later[...] = jnp.zeros_like(later)

    far_copy.wait()
    smooth_copy.wait()

    @pl.when(turn < turns - 1)
    def _():
        pltpu.make_async_copy(later, later, later_recv).wait()

    smooth_tile = square(m_full)
    matvec_loop(smooth_tile, [later[0], later[1]], [work.at[0], work.at[1]], blocks, blocks)
    second = jnp.where(core == 1, result_own[0], result_far[0])
    first_carried = second + work[0] + smooth_diag[...] * later[0]
    second_carried = later[0] + work[1] + smooth_diag[...] * later[1]
    work[0] = first_carried
    work[1] = second_carried
    part = pl.ds(core * (blocks // 2), blocks // 2)

    def half_tile(block, group):
        start = pl.multiple_of(core * half + block * LANES, LANES)
        return m_full[pl.ds(start, LANES), pl.ds(group * LANES, LANES)]

    matvec_loop(
        half_tile, [first_carried, second_carried], [summed.at[0], summed.at[1]], blocks // 2, blocks
    )
    diag_part = smooth_diag[part, :]
    for index in range(2):
        mean = jnp.where(core == index, result_own[1, part, :], result_far[1, part, :])
        late = mean + summed[index] + diag_part * work[index, part, :]
        for column in range(blocks // 2):
            columns = pl.ds(column * LANES, LANES)
            result[index : index + 1, columns] = mean[column : column + 1, :]
            result[index + 2 : index + 3, columns] = late[column : column + 1, :]

    @pl.when(leads | (follows & (place < group - 1)))
    def _():
        for block in range(chunks):
            for copy in block_copies(block):
                copy.wait_send()
        offset_copy.wait_send()

    @pl.when(sends_one)
    def _():
        for copy in chain_copies(1):
            copy.wait_send()

    @pl.when(sends_all)
    def _():
        for copy in chain_copies(group):
            copy.wait_send()

    @pl.when(turn > 0)
    def _():
        later_copy(0).wait_send()
        later_copy(1).wait_send()


def shards(
    dims,
    init_mean,
    jac_skew,
    gain_diag,
    gain_cross,
    smooth_diag,
    smooth_cross,
    obs_values,
    obs_prec,
    obs_sensor,
    obs_block,
    sensor_step,
):
    width = jac_skew.shape[2]
    blocks = width // LANES
    obs_total = lax.axis_size(("tm", "row"))
    vmem = pl.BlockSpec(memory_space=pltpu.VMEM)
    hbm = pl.BlockSpec(memory_space=pltpu.HBM)
    chunks = width // 2 // CHUNK
    group = dims[2]

    def wide(kind, lead=(), columns=width):
        return pltpu.VMEM(tuple(lead) + (width, columns), kind)

    def small(*lead):
        return pltpu.VMEM(tuple(lead) + (blocks, LANES), F32)

    dma = pltpu.SemaphoreType.DMA
    result = pl.pallas_call(
        functools.partial(kernel, dims),
        out_shape=jax.ShapeDtypeStruct((4, width // 2), F32),
        in_specs=[hbm, hbm, vmem, hbm] + [vmem] * 7,
        out_specs=vmem,
        scratch_shapes=[
            wide(BF16),
            wide(BF16),
            wide(BF16),
            wide(BF16),
            wide(BF16),
            wide(BF16),
            wide(BF16),
            wide(F32),
            wide(F32),
            wide(BF16),
            wide(BF16),
            wide(F32),
            wide(BF16, (2,)),
            wide(BF16, (2,)),
            wide(F32, (), width // 2),
            wide(BF16),
            wide(BF16),
            wide(F32, (), width // 2),
            pltpu.VMEM((chunks, CHUNK, width), jnp.int16),
            pltpu.VMEM((chunks, CHUNK, width), jnp.int16),
            pltpu.VMEM((chunks, 2, width), F32),
            pltpu.VMEM((chunks, 2, width), F32),
            pltpu.VMEM((LANES, width), F32),
            pltpu.VMEM((LANES, width), F32),
            pltpu.VMEM((obs_total, 2, LANES), F32),
            pltpu.VMEM((blocks, width), F32),
            small(2),
            small(2),
            small(2),
            small(),
            small(),
            small(),
            small(),
            small(2),
            small(),
            small(),
            small(2),
            small(2),
            small(2),
            small(2),
            pltpu.VMEM((2, blocks // 2, LANES), F32),
            dma((3,)),
            dma((2,)),
            dma((2, 2)),
            dma((10,)),
            dma((10,)),
            dma((2, 2)),
            dma((chunks, 2)),
            dma((chunks, 2)),
            dma((2,)),
            dma((2,)),
            dma((2 * group,)),
            dma,
            dma((3,)),
            dma,
            dma,
        ],
        compiler_params=pltpu.CompilerParams(
            collective_id=0, has_side_effects=True, vmem_limit_bytes=VMEM_BYTES
        ),
    )(
        jac_skew,
        gain_cross,
        gain_diag.reshape(blocks, LANES),
        smooth_cross,
        smooth_diag.reshape(blocks, LANES),
        init_mean.reshape(blocks, LANES),
        obs_values,
        obs_prec.reshape(1, 1),
        obs_sensor.reshape(1, 1),
        obs_block.reshape(1, 1),
        sensor_step.reshape(-1, LANES),
    )
    return result[:2], result[2:]


def solution(mesh):
    turns = mesh.shape["tm"]
    dims = {64: (4, 4, 4), 4: (1, 2, 2), 8: (2, 2, 2)}[turns]
    in_specs = (
        P(),
        P("tm", "row", None),
        P(),
        P(),
        P(),
        P(),
        P(("tm", "row"), None),
        P(("tm", "row")),
        P(("tm", "row")),
        P(("tm", "row")),
        P(),
    )
    out_specs = (P("tm", "row"), P("tm", "row"))
    return jax.shard_map(
        functools.partial(shards, dims),
        mesh=mesh,
        in_specs=in_specs,
        out_specs=out_specs,
        check_vma=False,
    )
```
